128 devices in a mesh: dp: 8 (over y, core), expert: 16 (over z, x).
Axes of the slice: x: 4, y: 4, z: 4, core: 2. Of those that a mesh axis runs over, the one named last changes fastest.
Arguments:
- tokens: bfloat16 [2048, 4096], P('expert', 'dp'), may hold values from -6 to 6
- grad_out: bfloat16 [2048, 4096], P('expert', 'dp'), may hold values from -6 to 6
- expert_ids: int32 [2048, 8], P('expert'), may hold values from 0 to 63, all different within a row; in each aligned block of 128 rows (0 to 127, 128 to 255, ...) at most 24 rows name the same one
- gate_probs: float32 [2048, 8], P('expert'), may hold values from 0.05 to 0.3
- seq_ids: int32 [2048], P('expert'), may hold values from 0 to 7, never falling along the last dimension, each value on 1 to 1024 neighbouring positions
- log_ratio: float32 [2048], P('expert'), may hold values from -8 to 8
- advantages: float32 [8], replicated, may hold values from -4 to 4
- w_gate: bfloat16 [64, 1536, 4096], P('expert', 'dp'), may hold values from -0.09375 to 0.09375
- w_up: bfloat16 [64, 1536, 4096], P('expert', 'dp'), may hold values from -0.09375 to 0.09375
- w_down: bfloat16 [64, 1536, 4096], P('expert', 'dp'), may hold values from -0.09375 to 0.09375
Outputs:
- grad_tokens: bfloat16 [2048, 4096], P('expert', 'dp')
- grad_gates: float32 [2048, 8], P('expert')
- grad_down: bfloat16 [64, 1536, 4096], P('expert', 'dp')
The draws below stay inside these ranges and needn't reach their ends.
Inputs may be any that keep to these rules, and one draw needn't show every extreme that they name: `expert_ids`: each row names 8 different experts; among the rows of one index of expert no expert is named more than 24 times, a bound that some block reaches. `seq_ids`: never falling; every sequence has 1 to 1024 tokens and one has exactly 1024.
All inputs are finite; a program needn't handle non-finite values.
Results may differ from the reference program's by a relative error of at most 0.023.
Values may be sent and summed in bfloat16 or wider, within the bound.
A program may use at most 192 MiB of HBM per device.

```python
import math
import jax
import jax.numpy as jnp
import numpy as np
from jax import lax

D = 4096
FF = 1536
TOP = 8
SEQS = 8
TOK_DEV = 128
EXPERTS = 64
TOKENS = 2048
CAP = 24
N_DP = 8
N_EXPERT = 16


def steps_of(own_key, shape, pieces, low, top_value):
    gain, own = 1.0, jax.random.fold_in(own_key, 6)
    for dim, blocks in pieces:
        draws = jnp.exp(jax.random.uniform(jax.random.fold_in(own, dim), (blocks,), jnp.float32, low / len(pieces), top_value / len(pieces)))
        gain = gain * jnp.repeat(draws, shape[dim] // blocks).reshape([-1 if axis == dim else 1 for axis in range(len(shape))])
    return gain


def split_up(count, total, most, skew):
    loads = [(1 << 20) // math.isqrt(grade ** skew) + 1 for grade in range(2, count + 1)]
    rest, given = total - most - (count - 1), [1] * (count - 1)
    while rest > 0:
        free = [i for i in range(count - 1) if given[i] < most]
        whole, budget = sum([loads[i] for i in free]), rest
        for i in free:
            extra = min(most - given[i], max(1, budget * loads[i] // whole), rest)
            given[i] = given[i] + extra
            rest = rest - extra
    return np.array([most] + given)


def ragged_sizes(stream_key, amount, total, reach, slope):
    if amount == 2:
        one = jax.random.randint(stream_key, (), max(1, total - reach), min(reach, total - 1) + 1)
        return jnp.stack([one, total - one])
    tallies = jnp.asarray(split_up(amount, total, reach, slope), jnp.int32)
    twos = (amount - 1) // 2
    donor, sink = tallies[1:1 + 2 * twos:2], tallies[2:2 + 2 * twos:2]
    slack = jnp.minimum(donor - 1, reach - sink)
    moved = jax.random.randint(jax.random.fold_in(stream_key, 1), (twos,), 0, 1 << 20) % (slack + 1)
    tallies = tallies.at[1:1 + 2 * twos:2].set(donor - moved).at[2:2 + 2 * twos:2].set(sink + moved)
    return tallies[jax.random.permutation(jax.random.fold_in(stream_key, 2), amount)]


def routed_block(key, own, number, rows, amount, top, bound, slope):
    sequence = jax.random.permutation(key, amount)
    heavy_load, usual = load_shares(amount, rows * top, bound, slope, True), load_shares(amount, rows * top, bound, slope, False)
    places = jnp.arange(amount)

    def named(tallies, rotation):
        used = int((tallies > 0).sum())
        fixed = max(1, used // 4)
        passed = fixed + (places - fixed + rotation * (used - fixed)) % max(1, amount - fixed)
        return jnp.zeros((amount,), jnp.int32).at[sequence[jnp.where(places < fixed, places, passed)]].set(jnp.asarray(tallies, jnp.int32))

    tallies = jnp.where(number % 4 == 0, named(heavy_load, number // 4), named(usual, number - number // 4 - 1))
    mixed = jax.random.permutation(jax.random.fold_in(own, 3), amount)
    source_of, receiver = mixed[0:amount // 2 * 2:2], mixed[1:amount // 2 * 2:2]
    slack = jnp.minimum(tallies[source_of] - 1, bound - tallies[receiver]) // 2
    slack = jnp.where((source_of == sequence[0]) | (receiver == sequence[0]) | (tallies[receiver] == 0), 0, jnp.maximum(slack, 0))
    passed = jax.random.randint(jax.random.fold_in(own, 4), (amount // 2,), 0, 1 << 20) % (slack + 1)
    tallies = tallies.at[source_of].add(-passed).at[receiver].add(passed)
    items = jnp.searchsorted(jnp.cumsum(tallies), jnp.arange(rows * top), side="right").astype(jnp.int32)
    table = items.reshape(top, rows).T
    table = table[jax.random.permutation(jax.random.fold_in(own, 1), rows)]
    rotation = jax.random.randint(jax.random.fold_in(own, 2), (rows, 1), 0, top)
    return jnp.take_along_axis(table, (jnp.arange(top)[None, :] + rotation) % top, axis=1)


def load_shares(number_of, total, bound, lean, full):
    weights = [(1 << 20) // math.isqrt(rank ** lean) + 1 for rank in range(1, number_of + 1)]
    largest = bound if full else min(bound, max(-(-total // number_of), total * weights[0] // sum(weights)))
    least = 1 if total - largest >= number_of - 1 else 0
    holding, surplus = [largest] + [least] * (number_of - 1), total - largest - least * (number_of - 1)
    while surplus > 0:
        candidates = [i for i in range(1, number_of) if holding[i] < largest] or [i for i in range(1, number_of) if holding[i] < bound]
        mass, left = sum([weights[i] for i in candidates]), surplus
        for i in candidates:
            addition = min(bound - holding[i], max(1, left * weights[i] // mass), surplus)
            holding[i] = holding[i] + addition
            surplus = surplus - addition
    return np.array(holding)


def centred(stream_key, dims, scale, most, cuts=(), held_as=jnp.bfloat16):
    entries = jax.random.normal(stream_key, dims, jnp.float32) * scale
    if len(cuts) > 0:
        entries = steps_of(stream_key, dims, cuts, -0.22, 0.18) * entries
    return jnp.clip(entries, min=-most, max=most).astype(held_as)


def setup_inputs(seed: int = 0) -> dict:
    seeds = jax.random.split(jax.random.key(seed), 11)
    tokens = centred(seeds[0], (TOKENS, D), 1.0, 6.0, ((0, 16), (1, 8)))
    grad_out = centred(seeds[1], (TOKENS, D), 1.0, 6.0, ((0, 16), (1, 8)))
    expert_ids_keys = jax.random.split(jax.random.fold_in(seeds[2], 1), TOKENS // TOK_DEV)
    expert_ids_turns = jax.random.permutation(jax.random.fold_in(seeds[2], 3), TOKENS // TOK_DEV)
    expert_ids = jax.vmap(lambda own, number: routed_block(jax.random.fold_in(seeds[2], 2), own, number, TOK_DEV, EXPERTS, TOP, CAP, 2))(expert_ids_keys, expert_ids_turns).reshape((TOKENS, TOP))
    gate_probs = jnp.clip(0.05 + 0.25 * jax.random.uniform(seeds[3], (TOKENS, TOP), jnp.float32) ** steps_of(seeds[3], (TOKENS, TOP), ((0, 16),), -0.2, 0.2), 0.05, 0.3)
    seq_ids = jnp.searchsorted(jnp.cumsum(ragged_sizes(seeds[4], SEQS, TOKENS, TOKENS // 2, 2)), jnp.arange(TOKENS), side="right").astype(jnp.int32)
    log_ratio = centred(seeds[5], (TOKENS,), 2.0, 8.0, ((0, 16),), jnp.float32)
    advantages = centred(seeds[6], (SEQS,), 1.0, 4.0, (), jnp.float32)
    w_gate = centred(seeds[7], (EXPERTS, FF, D), D ** -0.5, 0.09375, ((0, 16), (1, 8)))
    w_up = centred(seeds[8], (EXPERTS, FF, D), D ** -0.5, 0.09375, ((0, 16), (1, 8)))
    w_down = centred(seeds[9], (EXPERTS, FF, D), D ** -0.5, 0.09375, ((0, 16), (1, 8)))
    return {"tokens": tokens, "grad_out": grad_out, "expert_ids": expert_ids, "gate_probs": gate_probs, "seq_ids": seq_ids, "log_ratio": log_ratio, "advantages": advantages, "w_gate": w_gate, "w_up": w_up, "w_down": w_down}


clip_low = 0.9
clip_high = 1.1


def reference(tokens, grad_out, expert_ids, gate_probs, seq_ids, log_ratio, advantages, w_gate, w_up, w_down):
    onehot_seq = (seq_ids[:, None] == jnp.arange(SEQS, dtype=jnp.int32)[None, :]).astype(jnp.float32)
    sums = jnp.dot(log_ratio, onehot_seq, precision=lax.Precision.HIGHEST)
    counts = jnp.sum(onehot_seq, axis=0)
    clipped = jnp.clip(jnp.exp(sums / counts), clip_low, clip_high)
    seq_weight = advantages * clipped
    token_weight = jnp.dot(onehot_seq, seq_weight, precision=lax.Precision.HIGHEST)
    coef = token_weight[:, None] * gate_probs
    routes = TOKENS * TOP
    flat_ids = expert_ids.reshape(-1).astype(jnp.int32)
    token_of = (jnp.arange(routes, dtype=jnp.int32) // TOP).astype(jnp.int32)
    tokens_pad = jnp.concatenate([tokens, jnp.zeros((1, D), tokens.dtype)], axis=0)
    grads_pad = jnp.concatenate([grad_out, jnp.zeros((1, D), grad_out.dtype)], axis=0)
    coef_pad = jnp.concatenate([coef.reshape(-1), jnp.zeros((1,), jnp.float32)], axis=0)
    token_pad = jnp.concatenate([token_of, jnp.array([TOKENS], jnp.int32)], axis=0)
    most_rows = N_EXPERT * CAP
    group = FF // N_DP

    def one_expert(carry, expert):
        acc_dx, acc_gate = carry
        route_idx = jnp.nonzero(flat_ids == expert, size=most_rows, fill_value=routes)[0].astype(jnp.int32)
        tok_idx = token_pad[route_idx]
        xs = tokens_pad[tok_idx]
        dys = grads_pad[tok_idx]
        cs = coef_pad[route_idx]
        wg = w_gate[expert]
        wu = w_up[expert]
        wd = w_down[expert]
        g = jnp.dot(xs, wg.T, preferred_element_type=jnp.float32)
        u = jnp.dot(xs, wu.T, preferred_element_type=jnp.float32)
        sg = jax.nn.sigmoid(g)
        hidden = (g * sg * u).astype(jnp.bfloat16)
        z = jnp.dot(dys, wd.T, preferred_element_type=jnp.float32)
        dh = cs[:, None] * z
        dg = (dh * u * sg * (1.0 + g * (1.0 - sg))).astype(jnp.bfloat16)
        du = (dh * g * sg).astype(jnp.bfloat16)
        scaled = (cs[:, None] * dys.astype(jnp.float32)).astype(jnp.bfloat16)
        gdown = jnp.dot(hidden.T, scaled, preferred_element_type=jnp.float32).astype(jnp.bfloat16)
        dgr = dg.reshape(most_rows, N_DP, group).astype(jnp.float32)
        dur = du.reshape(most_rows, N_DP, group).astype(jnp.float32)
        wgr = wg.reshape(N_DP, group, D).astype(jnp.float32)
        wur = wu.reshape(N_DP, group, D).astype(jnp.float32)
        part = jnp.einsum('rjf,jfd->rjd', dgr, wgr) + jnp.einsum('rjf,jfd->rjd', dur, wur)
        slot_dx = jnp.sum(part.astype(jnp.bfloat16).astype(jnp.float32), axis=1)
        slot_gate = jnp.sum(hidden.astype(jnp.float32) * z, axis=1)
        acc_dx = acc_dx.at[tok_idx].add(slot_dx)
        acc_gate = acc_gate.at[route_idx].add(slot_gate)
        return (acc_dx, acc_gate), gdown

    start = (jnp.zeros((TOKENS + 1, D), jnp.float32), jnp.zeros((routes + 1,), jnp.float32))
    (acc_dx, acc_gate), grad_down = lax.scan(one_expert, start, jnp.arange(EXPERTS, dtype=jnp.int32))
    grad_tokens = acc_dx[:TOKENS].astype(jnp.bfloat16)
    grad_gates = token_weight[:, None] * acc_gate[:routes].reshape(TOKENS, TOP)
    return (grad_tokens, grad_gates, grad_down)
```

```python
import jax
import jax.numpy as jnp
from jax import lax
from jax.experimental import pallas as pl
from jax.experimental.pallas import tpu as pltpu
from jax.sharding import PartitionSpec as P

SEQS = 8
TOP = 8
CAP = 24
clip_low = 0.9
clip_high = 1.1

MESH = pl.DeviceIdType.MESH
BF = jnp.bfloat16
F32 = jnp.float32
PARTS = ((0, 176, 96), (176, 176, 80), (352, 160, 80))
ORDER = ((0, 1, 2), (1, 2, 0), (2, 0, 1))
BASE = (0, 1, 5)
COUNT = (1, 4, 16)
NT = (((1,), (1,)), ((), ()))
TN = (((0,), (0,)), ((), ()))


def group(a, b):
    return b * 4 + a


def step_kernel(
    adv, tok, gout, meta, wg, wu, wd,
    dxo, gates, gd,
    G, XS, DY, W, OWN, SND, RCV, DGU, HID, PM, CC, META, GROW, GS, GR, GT, GX,
    locsem, fs, fr, hs, hr, rfs, rfr, rhs, rhr, wl, ws, wr, ms, mr,
    es, er, ts, tr, gs1, gr1, gs2, gr2, ol, osnd, orcv, ready,
):
    dp = lax.axis_index("dp")
    ex = lax.axis_index("expert")
    pos = [ex % 4, dp // 2, ex // 4]
    core = dp % 2

    def dev(q, c):
        return (q[1] * 2 + c, q[2] * 4 + q[0])

    def shift(q, a, n):
        q = list(q)
        q[a] = (q[a] + n) % 4
        return q

    def blk(q):
        return (q[2] * 4 + q[0]) * 4 + q[1]

    nbr = [(dev(shift(pos, a, 1), core), dev(shift(pos, a, 3), core)) for a in range(3)]
    partner = (pos[1] * 2 + 1 - core, ex)
    me = blk(pos)
    bar = pltpu.get_barrier_semaphore()
    for i in range(1, 16):
        pl.semaphore_signal(bar, inc=1, device_id=(dp, (ex + i) % 16), device_id_type=MESH)
    for i in range(1, 8):
        pl.semaphore_signal(bar, inc=1, device_id=((dp + i) % 8, ex), device_id_type=MESH)

    loc = []
    for c in range(4):
        for w, src in enumerate((tok, gout)):
            loc.append(pltpu.make_async_copy(
                src.at[:, pl.ds(c * 128, 128)], G.at[w, me, pl.ds(c * 128, 128)], locsem.at[2 * c + w]))
    loc.append(pltpu.make_async_copy(meta, META.at[ex], locsem.at[8]))
    for l in loc:
        l.start()
    wcopies = []
    for k, (src, r0, r1) in enumerate(((wg, 0, 384), (wu, 192, 576), (wd, 768, 960))):
        for y in range(4):
            mine = pl.multiple_of(y * 1024 + core * 512, 512)
            theirs = pl.multiple_of(y * 1024 + (1 - core) * 512, 512)
            i = k * 4 + y
            wcopies.append(pltpu.make_async_copy(
                src.at[:, :, pl.ds(mine, 512)], W.at[:, pl.ds(r0, 192), pl.ds(y * 512, 512)], wl.at[i]))
            wcopies.append(pltpu.make_async_remote_copy(
                src.at[:, :, pl.ds(theirs, 512)], W.at[:, pl.ds(r1, 192), pl.ds(y * 512, 512)],
                ws.at[i], wr.at[i], partner, device_id_type=MESH))
    pl.semaphore_wait(bar, 22)
    for l in loc:
        l.wait()

    def origin(s, p, j):
        q = list(pos)
        o = ORDER[p]
        if s >= 1:
            q = shift(q, o[0], j % 4)
        if s == 2:
            q = shift(q, o[1], j // 4)
        return q

    def sem_at(p, s, j, way):
        return (p * 21 + BASE[s] + j) * 2 + way

    def half_rows(p, way):
        r0, n, h = PARTS[p]
        return pl.ds(r0, h) if way == 0 else pl.ds(r0 + h, n - h)

    def part_rows(p):
        return pl.ds(PARTS[p][0], PARTS[p][1])

    def full(v, s, p, j, way):
        i = v * 126 + sem_at(p, s, j, way)
        ref = G.at[v, blk(origin(s, p, j)), part_rows(p)]
        return pltpu.make_async_remote_copy(
            ref, ref, fs.at[i], fr.at[i], nbr[ORDER[p][s]][way], device_id_type=MESH)

    def half(v, s, p, j, way):
        a = ORDER[p][s]
        i = v * 126 + sem_at(p, s, j, way)
        k = blk(shift(origin(s, p, j), a, 3 if way == 0 else 1))
        ref = G.at[v, k, half_rows(p, way)]
        return pltpu.make_async_remote_copy(
            ref, ref, hs.at[i], hr.at[i], nbr[a][way], device_id_type=MESH)

    def each(f):
        for p in range(3):
            for way in range(2):
                f(p, way)

    def odd(f):
        def body(i, c):
            f(1 + 2 * i)
            return c
        lax.fori_loop(0, 2, body, 0)

    def send(v, s, j):
        each(lambda p, w: full(v, s, p, j, w).start())

    def hop(v, s, j):
        def one(p, w):
            full(v, s, p, j, w).wait_recv()
            half(v, s, p, j, w).start()
        each(one)

    def last(v, s, j):
        each(lambda p, w: half(v, s, p, j, w).wait_recv())

    def gather_events(v):
        ev = []
        ev.append(lambda: (send(v, 0, 0), send(v, 1, 0), send(v, 2, 0)))
        ev.append(lambda: (hop(v, 0, 0), odd(lambda a: send(v, 1, a)), odd(lambda a: send(v, 2, group(a, 0)))))
        ev.append(lambda: (hop(v, 1, 0), odd(lambda b: send(v, 2, group(0, b))), hop(v, 2, 0)))
        ev.append(lambda: (last(v, 0, 0), send(v, 1, 2), send(v, 2, group(2, 0))))
        ev.append(lambda: odd(lambda a: (hop(v, 1, a), odd(lambda b: send(v, 2, group(a, b))))))
        ev.append(lambda: (last(v, 1, 0), send(v, 2, group(0, 2))))
        ev.append(lambda: (odd(lambda a: hop(v, 2, group(a, 0))), odd(lambda b: hop(v, 2, group(0, b)))))
        ev.append(lambda: (hop(v, 1, 2), odd(lambda b: send(v, 2, group(2, b)))))
        ev.append(lambda: odd(lambda a: (last(v, 1, a), send(v, 2, group(a, 2)))))
        ev.append(lambda: (hop(v, 2, group(2, 0)), odd(lambda a: odd(lambda b: hop(v, 2, group(a, b))))))
        ev.append(lambda: hop(v, 2, group(0, 2)))
        ev.append(lambda: (last(v, 1, 2), send(v, 2, group(2, 2))))
        ev.append(lambda: (odd(lambda b: hop(v, 2, group(2, b))), odd(lambda a: hop(v, 2, group(a, 2)))))
        ev.append(lambda: hop(v, 2, group(2, 2)))
        return ev

    def gather_rest(v):
        def fin(j, c):
            last(v, 2, j)
            return c
        lax.fori_loop(0, 16, fin, 0)

    def gather_sent(v):
        for s in range(3):
            def fin(j, c, s=s):
                def one(p, w):
                    full(v, s, p, j, w).wait_send()
                    half(v, s, p, j, w).wait_send()
                each(one)
                return c
            lax.fori_loop(0, COUNT[s], fin, 0)

    def meta_copy(i):
        return pltpu.make_async_remote_copy(
            META.at[ex], META.at[ex], ms.at[i], mr.at[i], (dp, (ex + i) % 16), device_id_type=MESH)

    first = (ex * 4).astype(F32)

    def pair_ids(q):
        return jnp.concatenate([META[2 * q, 0:8], META[2 * q + 1, 0:8]], axis=1)

    def prepare():
        sid = META[:, 16, :]
        lr = META[:, 17, :]
        tw = jnp.zeros((16, 128), F32)
        for s in range(SEQS):
            hit = (sid == float(s)).astype(F32)
            total = jnp.sum(jnp.sum(hit * lr, axis=1, keepdims=True), axis=0, keepdims=True)
            count = jnp.sum(jnp.sum(hit, axis=1, keepdims=True), axis=0, keepdims=True)
            wt = adv[s] * jnp.clip(jnp.exp(total / count), clip_low, clip_high)
            tw = tw + hit * wt
        r = lax.broadcasted_iota(jnp.int32, (256, 256), 0)
        t = lax.broadcasted_iota(jnp.int32, (256, 256), 1)
        earlier = ((r < t) & ((r >= 128) == (t >= 128))).astype(F32).astype(BF)
        row = lax.broadcasted_iota(jnp.int32, (2 * CAP, 256), 0)
        lane = lax.broadcasted_iota(jnp.int32, (2 * CAP, 256), 1)
        second = row >= CAP
        same = second == (lane >= 128)
        slot = (row - jnp.where(second, CAP, 0)).astype(F32)
        for q in range(8):
            ids = pair_ids(q)
            gp = jnp.concatenate([META[2 * q, 8:16], META[2 * q + 1, 8:16]], axis=1)
            twq = jnp.concatenate([tw[2 * q:2 * q + 1], tw[2 * q + 1:2 * q + 2]], axis=1)
            hot, cw = [], []
            for n in range(4):
                hit = (ids == first + float(n)).astype(F32)
                hot.append(jnp.sum(hit, axis=0, keepdims=True))
                cw.append(jnp.sum(hit * gp, axis=0, keepdims=True) * twq)
            hots = jnp.concatenate(hot + hot, axis=0)
            rank = jnp.dot(hots.astype(BF), earlier, preferred_element_type=F32)
            for n in range(4):
                sel = same & (rank[n:n + 1] == slot) & (hot[n] > 0.5)
                pick = sel.astype(F32)
                PM[q, n * 48:(n + 1) * 48, :] = pick.astype(BF)
                cc = jnp.sum(pick * cw[n], axis=1, keepdims=True)
                CC[q, n * 48:(n + 1) * 48, :] = jnp.broadcast_to(cc, (48, 128))

    def select(v, q):
        dst = XS if v == 0 else DY
        rows = pl.ds(pl.multiple_of(q * 48, 16), 48)
        pm = PM[q]
        for y in range(4):
            xp = jnp.concatenate([
                jnp.concatenate([G[v, (2 * q + b) * 4 + y, c * 128:(c + 1) * 128, :] for c in range(4)], axis=1)
                for b in range(2)], axis=0)
            r = jnp.dot(pm, xp, preferred_element_type=F32)
            if v == 1:
                r = r * CC[q, :, 0:1]
            r = r.astype(BF)
            for n in range(4):
                dst[n, rows, y * 512:(y + 1) * 512] = r[n * 48:(n + 1) * 48]

    def loop(lo, hi, f):
        def body(i, c):
            f(i)
            return c
        lax.fori_loop(lo, hi, body, 0)

    def swap_gu(n):
        return pltpu.make_async_remote_copy(
            SND.at[n, pl.ds(0, 384)], RCV.at[n, pl.ds(0, 384)], es.at[n], er.at[n], partner, device_id_type=MESH)

    def swap_z(n):
        return pltpu.make_async_remote_copy(
            SND.at[n, pl.ds(384, 192)], RCV.at[n, pl.ds(384, 192)], es.at[4 + n], er.at[4 + n], partner,
            device_id_type=MESH)

    def gate_up(n):
        x = XS[n]
        OWN[n, 0:384] = lax.dot_general(W[n, 0:384], x, NT, preferred_element_type=F32)
        SND[n, 0:384] = lax.dot_general(W[n, 384:768], x, NT, preferred_element_type=F32).astype(BF)
        swap_gu(n).start()

    def down(n):
        z = lax.dot_general(W[n, 768:1152], DY[n], NT, preferred_element_type=F32)
        OWN[n, 384:576] = z[0:192]
        SND[n, 384:576] = z[192:384].astype(BF)
        swap_z(n).start()

    def swap_d(n):
        return pltpu.make_async_remote_copy(
            DGU.at[n, pl.ds(0, 384)], DGU.at[n, pl.ds(384, 384)], ts.at[n], tr.at[n], partner, device_id_type=MESH)

    def swap_h(n):
        return pltpu.make_async_remote_copy(
            HID.at[n, pl.ds(0, 192)], HID.at[n, pl.ds(192, 192)], ts.at[4 + n], tr.at[4 + n], partner,
            device_id_type=MESH)

    def middle(n):
        swap_gu(n).wait_recv()
        swap_z(n).wait_recv()
        g = OWN[n, 0:192] + RCV[n, 0:192].astype(F32)
        u = OWN[n, 192:384] + RCV[n, 192:384].astype(F32)
        z = OWN[n, 384:576] + RCV[n, 384:576].astype(F32)
        sg = jax.nn.sigmoid(g)
        gsg = g * sg
        h = (gsg * u).astype(BF)
        DGU[n, 0:192] = (z * u * sg * (1.0 + g * (1.0 - sg))).astype(BF)
        DGU[n, 192:384] = (z * gsg).astype(BF)
        HID[n, 0:192] = h
        GROW[n] = jnp.broadcast_to(jnp.sum(h.astype(F32) * z, axis=0, keepdims=True), (8, 384))
        swap_d(n).start()
        swap_h(n).start()

    def grad_x(n):
        swap_d(n).wait_recv()
        d = DGU[n].T
        for y in range(4):
            cols = slice(y * 512, (y + 1) * 512)
            XS[n, :, cols] = jnp.dot(d, W[n, 0:768, cols], preferred_element_type=F32).astype(BF)

    def scatter(q):
        rows = pl.ds(pl.multiple_of(q * 48, 16), 48)
        pt = PM[q].T
        for y in range(4):
            part = jnp.concatenate([XS[n, rows, y * 512:(y + 1) * 512] for n in range(4)], axis=0)
            r = jnp.dot(pt, part, preferred_element_type=F32).astype(BF)
            for b in range(2):
                for c in range(4):
                    G[0, (2 * q + b) * 4 + y, c * 128:(c + 1) * 128, :] = (
                        r[b * 128:(b + 1) * 128, c * 128:(c + 1) * 128])

    def out_local(n, y):
        cols = pl.multiple_of(y * 1024 + core * 512, 512)
        return pltpu.make_async_copy(
            XS.at[n, pl.ds(0, 192), pl.ds(y * 512, 512)], gd.at[n, :, pl.ds(cols, 512)], ol.at[n * 4 + y])

    def out_remote(n, y):
        cols = pl.multiple_of(y * 1024 + core * 512, 512)
        return pltpu.make_async_remote_copy(
            XS.at[n, pl.ds(192, 192), pl.ds(y * 512, 512)], gd.at[n, :, pl.ds(cols, 512)],
            osnd.at[n * 4 + y], orcv.at[n * 4 + y], partner, device_id_type=MESH)

    def grad_down(n):
        swap_h(n).wait_recv()
        h = HID[n]
        for y in range(4):
            cols = slice(y * 512, (y + 1) * 512)
            XS[n, :, cols] = jnp.dot(h, DY[n, :, cols], preferred_element_type=F32).astype(BF)
            out_local(n, y).start()
            out_remote(n, y).start()

    def gate_tokens():
        lane = lax.broadcasted_iota(jnp.int32, (8, 192), 1)
        row = lax.broadcasted_iota(jnp.int32, (8, 192), 0)
        own = (lane >= row * 48) & (lane < row * 48 + 48)
        for q in range(8):
            vals = jnp.concatenate([GROW[n, 0:1, q * 48:(q + 1) * 48] for n in range(4)], axis=1)
            a = jnp.where(own, vals, 0.0)
            gt = jnp.dot(a, PM[q].astype(F32), precision=lax.Precision.HIGHEST, preferred_element_type=F32)
            ids = pair_ids(q)
            r = jnp.zeros((8, 256), F32)
            for n in range(4):
                r = r + jnp.where(ids == first + float(n), gt[n:n + 1], 0.0)
            GS[2 * q] = r[:, 0:128]
            GS[2 * q + 1] = r[:, 128:256]

    def gate_one(i):
        e = (ex + i) % 16
        return pltpu.make_async_remote_copy(
            GS.at[e], GR.at[i], gs1.at[i], gr1.at[i], (dp, e), device_id_type=MESH)

    def gate_two(i):
        return pltpu.make_async_remote_copy(
            GT, GX.at[i], gs2.at[i], gr2.at[i], ((dp + i) % 8, ex), device_id_type=MESH)

    def rhalf(s, p, j, way):
        a = ORDER[p][s]
        i = sem_at(p, s, j, way)
        k = blk(shift(origin(s, p, j), a, 2))
        rows = half_rows(p, way)
        return pltpu.make_async_remote_copy(
            G.at[0, k, rows], G.at[1, BASE[s] + j, rows], rhs.at[i], rhr.at[i], nbr[a][way], device_id_type=MESH)

    def rfull(s, p, j, way):
        a = ORDER[p][s]
        i = sem_at(p, s, j, way)
        k = blk(shift(origin(s, p, j), a, 1 if way == 0 else 3))
        rows = part_rows(p)
        return pltpu.make_async_remote_copy(
            G.at[0, k, rows], G.at[1, 21 + (BASE[s] + j) * 2 + way, rows], rfs.at[i], rfr.at[i], nbr[a][way],
            device_id_type=MESH)

    def r_start(s, j):
        each(lambda p, w: rhalf(s, p, j, w).start())

    def r_mid(s, j):
        def one(p, way):
            rhalf(s, p, j, way).wait_recv()
            k = blk(shift(origin(s, p, j), ORDER[p][s], 1 if way == 0 else 3))
            rows = half_rows(p, way)
            G[0, k, rows] = (G[0, k, rows].astype(F32) + G[1, BASE[s] + j, rows].astype(F32)).astype(BF)
            rfull(s, p, j, way).start()
        each(one)

    def r_end(s, j):
        for p in range(3):
            for way in range(2):
                rfull(s, p, j, way).wait_recv()
            k = blk(origin(s, p, j))
            rows = part_rows(p)
            f = 21 + (BASE[s] + j) * 2
            G[0, k, rows] = (G[0, k, rows].astype(F32) + (
                G[1, f, rows].astype(F32) + G[1, f + 1, rows].astype(F32))).astype(BF)

    def r_sent():
        for s in range(3):
            def fin(j, c, s=s):
                def one(p, w):
                    rhalf(s, p, j, w).wait_send()
                    rfull(s, p, j, w).wait_send()
                each(one)
                return c
            lax.fori_loop(0, COUNT[s], fin, 0)

    far = (2, 3, 1, 0)
    for i in range(1, 16):
        meta_copy(i).start()
    ev0 = gather_events(0)
    ev0[0]()
    for c in wcopies:
        c.start()
    for i in range(1, 16):
        meta_copy(i).wait()
    ev0[1]()
    ev0[2]()
    prepare()
    for e in ev0[3:]:
        e()
    ev1 = gather_events(1)
    ev1[0]()
    gather_rest(0)
    ev1[1]()
    ev1[2]()
    ev1[3]()
    loop(0, 4, lambda q: select(0, q))
    ev1[4]()
    ev1[5]()
    ev1[6]()
    loop(4, 8, lambda q: select(0, q))
    for c in wcopies:
        c.wait()
    ev1[7]()
    ev1[8]()
    ev1[9]()
    loop(0, 2, gate_up)
    for e in ev1[10:]:
        e()
    loop(2, 4, gate_up)
    gather_rest(1)
    loop(0, 8, lambda q: select(1, q))
    gather_sent(0)
    gather_sent(1)
    for a in range(3):
        for n in nbr[a]:
            pl.semaphore_signal(ready, inc=1, device_id=n, device_id_type=MESH)
    loop(0, 4, down)
    loop(0, 4, middle)
    loop(0, 4, grad_x)
    loop(0, 8, scatter)
    pl.semaphore_wait(ready, 6)
    for b in far:
        loop(0, 4, lambda a, b=b: r_start(2, group((a + 2) % 4, b)))
    gate_tokens()
    for i in range(1, 16):
        gate_one(i).start()
    for b in far:
        loop(0, 4, lambda a, b=b: r_mid(2, group((a + 2) % 4, b)))
    loop(0, 4, grad_down)
    for i in range(1, 16):
        gate_one(i).wait()
    acc = GS[ex]
    for i in range(1, 16):
        acc = acc + GR[i]
    GT[...] = acc
    for i in range(1, 8):
        gate_two(i).start()
    for a in far:
        r_end(2, group(a, 2))
        r_start(1, a)
    for a in far:
        r_end(2, group(a, 1))
        r_end(2, group(a, 3))
        r_mid(1, a)
    r_end(2, group(2, 0))
    r_end(1, 2)
    r_start(0, 0)
    for a in (1, 3):
        r_end(2, group(a, 0))
        r_end(1, a)
    r_mid(0, 0)
    r_end(2, 0)
    r_end(1, 0)
    r_end(0, 0)
    for c in range(4):
        dxo[:, c * 128:(c + 1) * 128] = G[0, me, c * 128:(c + 1) * 128, :]
    for i in range(1, 8):
        gate_two(i).wait()
    acc = GT[...]
    for i in range(1, 8):
        acc = acc + GX[i]
    gates[...] = acc
    r_sent()

    def finish(n):
        swap_gu(n).wait_send()
        swap_z(n).wait_send()
        swap_d(n).wait_send()
        swap_h(n).wait_send()
        for y in range(4):
            out_local(n, y).wait()
            out_remote(n, y).wait()
    loop(0, 4, finish)


def on_device(
    tokens, grad_out, expert_ids, gate_probs, seq_ids, log_ratio, advantages, w_gate, w_up, w_down
):
    meta = jnp.concatenate([
        expert_ids.astype(F32).T, gate_probs.T, seq_ids.astype(F32)[None], log_ratio[None],
        jnp.zeros((6, 128), F32)], axis=0)
    vmem = pl.BlockSpec(memory_space=pltpu.VMEM)
    hbm = pl.BlockSpec(memory_space=pl.ANY)
    dma = lambda n: pltpu.SemaphoreType.DMA((n,))
    dx, gates, gd = pl.pallas_call(
        step_kernel,
        out_shape=(
            jax.ShapeDtypeStruct((128, 512), BF),
            jax.ShapeDtypeStruct((8, 128), F32),
            jax.ShapeDtypeStruct((4, 192, 4096), BF),
        ),
        in_specs=[pl.BlockSpec(memory_space=pltpu.SMEM), vmem, vmem, vmem, hbm, hbm, hbm],
        out_specs=(vmem, vmem, hbm),
        scratch_shapes=[
            pltpu.VMEM((2, 64, 512, 128), BF),
            pltpu.VMEM((4, 384, 2048), BF),
            pltpu.VMEM((4, 384, 2048), BF),
            pltpu.VMEM((4, 1152, 2048), BF),
            pltpu.VMEM((4, 576, 384), F32),
            pltpu.VMEM((4, 576, 384), BF),
            pltpu.VMEM((4, 576, 384), BF),
            pltpu.VMEM((4, 768, 384), BF),
            pltpu.VMEM((4, 384, 384), BF),
            pltpu.VMEM((8, 192, 256), BF),
            pltpu.VMEM((8, 192, 128), F32),
            pltpu.VMEM((16, 24, 128), F32),
            pltpu.VMEM((4, 8, 384), F32),
            pltpu.VMEM((16, 8, 128), F32),
            pltpu.VMEM((16, 8, 128), F32),
            pltpu.VMEM((8, 128), F32),
            pltpu.VMEM((8, 8, 128), F32),
            dma(9), dma(252), dma(252), dma(252), dma(252), dma(126), dma(126), dma(126), dma(126),
            dma(12), dma(12), dma(12), dma(16), dma(16),
            dma(8), dma(8), dma(8), dma(8), dma(16), dma(16), dma(8), dma(8), dma(16), dma(16), dma(16),
            pltpu.SemaphoreType.REGULAR,
        ],
        compiler_params=pltpu.CompilerParams(
            collective_id=0, has_side_effects=True, vmem_limit_bytes=67043328),
        name="expert_step",
    )(advantages, tokens, grad_out, meta, w_gate, w_up, w_down)
    return dx, gates.T / gate_probs, gd


def solution(mesh):
    return jax.shard_map(
        on_device,
        mesh=mesh,
        in_specs=(
            P("expert", "dp"),
            P("expert", "dp"),
            P("expert", None),
            P("expert", None),
            P("expert"),
            P("expert"),
            P(),
            P("expert", "dp", None),
            P("expert", "dp", None),
            P("expert", "dp", None),
        ),
        out_specs=(P("expert", "dp"), P("expert", None), P("expert", "dp", None)),
        check_vma=False,
    )
```

```python
import jax
import jax.numpy as jnp
from jax import lax
from jax.experimental import pallas as pl
from jax.experimental.pallas import tpu as pltpu
from jax.sharding import PartitionSpec as P

SEQS = 8
TOP = 8
CAP = 24
clip_low = 0.9
clip_high = 1.1

MESH = pl.DeviceIdType.MESH
BF = jnp.bfloat16
F32 = jnp.float32
PARTS = ((0, 176, 96), (176, 176, 80), (352, 160, 80))
ORDER = ((0, 1, 2), (1, 2, 0), (2, 0, 1))
BASE = (0, 1, 5)
COUNT = (1, 4, 16)
NT = (((1,), (1,)), ((), ()))
TN = (((0,), (0,)), ((), ()))


def group(a, b):
    return b * 4 + a


def step_kernel(
    adv, tok, gout, idt, gpt, seq, ratio, wg, wu, wd,
    dxo, gates, gd,
    G, XS, DY, W, OWN, SND, RCV, DT, HID, PM, PT, CC, META, GROW, GS, GR, GT, GX,
    locsem, sent, fr, hr, wl, ws, wr, ms, mr,
    es, er, ts, tr, th, gs1, gr1, gs2, gr2, ol, osnd, orcv, ready,
):
    dp = lax.axis_index("dp")
    ex = lax.axis_index("expert")
    pos = [ex % 4, dp // 2, ex // 4]
    core = dp % 2

    def dev(q, c):
        return (q[1] * 2 + c, q[2] * 4 + q[0])

    def shift(q, a, n):
        q = list(q)
        q[a] = (q[a] + n) % 4
        return q

    def blk(q):
        return (q[2] * 4 + q[0]) * 4 + q[1]

    nbr = [(dev(shift(pos, a, 1), core), dev(shift(pos, a, 3), core)) for a in range(3)]
    partner = (pos[1] * 2 + 1 - core, ex)
    me = blk(pos)
    bar = pltpu.get_barrier_semaphore()
    for i in range(1, 16):
        pl.semaphore_signal(bar, inc=1, device_id=(dp, (ex + i) % 16), device_id_type=MESH)
    for i in range(1, 8):
        pl.semaphore_signal(bar, inc=1, device_id=((dp + i) % 8, ex), device_id_type=MESH)

    def settle(ref, sem):
        pltpu.make_async_copy(ref, ref, sem).wait()

    for c in range(4):
        for w, src in enumerate((tok, gout)):
            pltpu.make_async_copy(
                src.at[:, pl.ds(c * 128, 128)], G.at[w, me, pl.ds(c * 128, 128)], locsem.at[w]).start()
    META[ex, 0:8, :] = idt[...].astype(F32)
    META[ex, 8:16, :] = gpt[...]
    META[ex, 16:17, :] = seq[...].astype(F32)
    META[ex, 17:18, :] = ratio[...]

    def fetch_weights():
        for k, (src, r0, r1) in enumerate(((wg, 0, 384), (wu, 192, 576), (wd, 768, 960))):
            for y in range(4):
                mine = pl.multiple_of(y * 1024 + core * 512, 512)
                theirs = pl.multiple_of(y * 1024 + (1 - core) * 512, 512)
                pltpu.make_async_copy(
                    src.at[:, :, pl.ds(mine, 512)], W.at[:, pl.ds(r0, 192), pl.ds(y * 512, 512)], wl.at[0]).start()
                pltpu.make_async_remote_copy(
                    src.at[:, :, pl.ds(theirs, 512)], W.at[:, pl.ds(r1, 192), pl.ds(y * 512, 512)],
                    ws.at[0], wr.at[0], partner, device_id_type=MESH).start()

    def settle_weights():
        for sem in (wl, ws, wr):
            settle(W.at[:, pl.ds(0, 576)], sem.at[0])

    pl.semaphore_wait(bar, 22)
    for w in range(2):
        settle(G.at[w, me], locsem.at[w])

    def origin(s, p, j):
        q = list(pos)
        o = ORDER[p]
        if s >= 1:
            q = shift(q, o[0], j % 4)
        if s == 2:
            q = shift(q, o[1], j // 4)
        return q

    def slot(s, k):
        return (0, 1, 5)[s] + k

    def full_sem(v, p, way, k):
        return ((v * 3 + p) * 2 + way) * 9 + k

    def half_sem(v, p, way, k):
        return ((v * 3 + p) * 2 + way) * 6 + k

    def sent_sem(v, p, way):
        return (v * 3 + p) * 2 + way

    def half_rows(p, way):
        r0, n, h = PARTS[p]
        return pl.ds(r0, h) if way == 0 else pl.ds(r0 + h, n - h)

    def part_rows(p):
        return pl.ds(PARTS[p][0], PARTS[p][1])

    def full(v, s, p, j, way):
        ref = G.at[v, blk(origin(s, p, j)), part_rows(p)]
        k = slot(s, j // 4 if s == 2 else j)
        return pltpu.make_async_remote_copy(
            ref, ref, sent.at[sent_sem(v, p, way)], fr.at[full_sem(v, p, way, k)], nbr[ORDER[p][s]][way],
            device_id_type=MESH)

    def half(v, s, p, j, way):
        a = ORDER[p][s]
        b = blk(shift(origin(s, p, j), a, 3 if way == 0 else 1))
        ref = G.at[v, b, half_rows(p, way)]
        k = 5 if s == 2 else slot(s, j)
        return pltpu.make_async_remote_copy(
            ref, ref, sent.at[sent_sem(v, p, way)], hr.at[half_sem(v, p, way, k)], nbr[a][way],
            device_id_type=MESH)

    def each(f):
        for p in range(3):
            for way in range(2):
                f(p, way)

    def odd(f):
        def body(i, c):
            f(1 + 2 * i)
            return c
        lax.fori_loop(0, 2, body, 0)

    def loop(lo, hi, f):
        def body(i, c):
            f(i)
            return c
        lax.fori_loop(lo, hi, body, 0)

    def send(v, s, j):
        each(lambda p, w: full(v, s, p, j, w).start())

    def hop(v, s, j):
        def one(p, w):
            full(v, s, p, j, w).wait_recv()
            half(v, s, p, j, w).start()
        each(one)

    def hop_bundle(v, b):
        for p in range(3):
            for w in range(2):
                settle(G.at[v, pl.ds(0, 4), part_rows(p)], fr.at[full_sem(v, p, w, slot(2, b))])
                loop(0, 4, lambda a, p=p, w=w: half(v, 2, p, group(a, b), w).start())

    def last(v, s, j):
        each(lambda p, w: half(v, s, p, j, w).wait_recv())

    def gather_events(v):
        ev = []
        ev.append(lambda: (send(v, 0, 0), send(v, 1, 0), send(v, 2, 0)))
        ev.append(lambda: (hop(v, 0, 0), odd(lambda a: send(v, 1, a)), odd(lambda a: send(v, 2, group(a, 0)))))
        ev.append(lambda: (hop(v, 1, 0), odd(lambda b: send(v, 2, group(0, b)))))
        ev.append(lambda: (last(v, 0, 0), send(v, 1, 2), send(v, 2, group(2, 0))))
        ev.append(lambda: odd(lambda a: (hop(v, 1, a), odd(lambda b: send(v, 2, group(a, b))))))
        ev.append(lambda: (last(v, 1, 0), send(v, 2, group(0, 2))))
        ev.append(lambda: hop_bundle(v, 0))
        ev.append(lambda: (hop(v, 1, 2), odd(lambda b: send(v, 2, group(2, b)))))
        ev.append(lambda: odd(lambda a: (last(v, 1, a), send(v, 2, group(a, 2)))))
        ev.append(lambda: (last(v, 1, 2), send(v, 2, group(2, 2))))
        ev.append(lambda: odd(lambda b: hop_bundle(v, b)))
        ev.append(lambda: hop_bundle(v, 2))
        return ev

    def gather_rest(v):
        def one(p, w):
            h = PARTS[p][2] if w == 0 else PARTS[p][1] - PARTS[p][2]
            settle(G.at[v, pl.ds(0, 16), pl.ds(0, h)], hr.at[half_sem(v, p, w, 5)])
        each(one)

    def all_sent(v):
        def one(p, w):
            h = PARTS[p][2] if w == 0 else PARTS[p][1] - PARTS[p][2]
            settle(G.at[v, pl.ds(0, 21), pl.ds(0, PARTS[p][1] + h)], sent.at[sent_sem(v, p, w)])
        each(one)

    def meta_copy(i):
        return pltpu.make_async_remote_copy(
            META.at[ex], META.at[ex], ms.at[0], mr.at[0], (dp, (ex + i) % 16), device_id_type=MESH)

    first = (ex * 4).astype(F32)

    def pair_ids(q):
        return jnp.concatenate([META[2 * q, 0:8], META[2 * q + 1, 0:8]], axis=1)

    def prepare():
        sid = META[:, 16, :]
        lr = META[:, 17, :]
        tw = jnp.zeros((16, 128), F32)
        for s in range(SEQS):
            hit = (sid == float(s)).astype(F32)
            total = jnp.sum(jnp.sum(hit * lr, axis=1, keepdims=True), axis=0, keepdims=True)
            count = jnp.sum(jnp.sum(hit, axis=1, keepdims=True), axis=0, keepdims=True)
            wt = adv[s] * jnp.clip(jnp.exp(total / count), clip_low, clip_high)
            tw = tw + hit * wt
        r = lax.broadcasted_iota(jnp.int32, (256, 256), 0)
        t = lax.broadcasted_iota(jnp.int32, (256, 256), 1)
        earlier = ((r < t) & ((r >= 128) == (t >= 128))).astype(F32).astype(BF)
        row = lax.broadcasted_iota(jnp.int32, (2 * CAP, 256), 0)
        lane = lax.broadcasted_iota(jnp.int32, (2 * CAP, 256), 1)
        second = row >= CAP
        same = second == (lane >= 128)
        slot = (row - jnp.where(second, CAP, 0)).astype(F32)
        for q in range(8):
            ids = pair_ids(q)
            gp = jnp.concatenate([META[2 * q, 8:16], META[2 * q + 1, 8:16]], axis=1)
            twq = jnp.concatenate([tw[2 * q:2 * q + 1], tw[2 * q + 1:2 * q + 2]], axis=1)
            hot, cw = [], []
            for n in range(4):
                hit = (ids == first + float(n)).astype(F32)
                hot.append(jnp.sum(hit, axis=0, keepdims=True))
                cw.append(jnp.sum(hit * gp, axis=0, keepdims=True) * twq)
            hots = jnp.concatenate(hot + hot, axis=0)
            rank = jnp.dot(hots.astype(BF), earlier, preferred_element_type=F32)
            for n in range(4):
                sel = same & (rank[n:n + 1] == slot) & (hot[n] > 0.5)
                pick = sel.astype(F32)
                PM[q, n * 48:(n + 1) * 48, :] = pick.astype(BF)
                cc = jnp.sum(pick * cw[n], axis=1, keepdims=True)
                CC[q, n * 48:(n + 1) * 48, :] = jnp.broadcast_to(cc, (48, 128))
            PT[q] = PM[q].T

    def select(v, q):
        dst = XS if v == 0 else DY
        rows = pl.ds(pl.multiple_of(q * 48, 16), 48)
        pm = PM[q]
        for y in range(4):
            xp = jnp.concatenate([
                jnp.concatenate([G[v, (2 * q + b) * 4 + y, c * 128:(c + 1) * 128, :] for c in range(4)], axis=1)
                for b in range(2)], axis=0)
            r = jnp.dot(pm, xp, preferred_element_type=F32)
            if v == 1:
                r = r * CC[q, :, 0:1]
            r = r.astype(BF)
            for n in range(4):
                dst[n, rows, y * 512:(y + 1) * 512] = r[n * 48:(n + 1) * 48]

    def swap_gu(n):
        return pltpu.make_async_remote_copy(
            SND.at[n, pl.ds(0, 384)], RCV.at[n, pl.ds(0, 384)], es.at[0], er.at[n], partner, device_id_type=MESH)

    def swap_z(n):
        return pltpu.make_async_remote_copy(
            SND.at[n, pl.ds(384, 192)], RCV.at[n, pl.ds(384, 192)], es.at[0], er.at[4 + n], partner,
            device_id_type=MESH)

    def gate_up(n):
        x = XS[n]
        OWN[n, 0:384] = lax.dot_general(W[n, 0:384], x, NT, preferred_element_type=F32)
        SND[n, 0:384] = lax.dot_general(W[n, 384:768], x, NT, preferred_element_type=F32).astype(BF)
        swap_gu(n).start()

    def down(n):
        z = lax.dot_general(W[n, 768:1152], DY[n], NT, preferred_element_type=F32)
        OWN[n, 384:576] = z[0:192]
        SND[n, 384:576] = z[192:384].astype(BF)
        swap_z(n).start()

    def swap_d(n):
        return pltpu.make_async_remote_copy(
            DT.at[n, :, pl.ds(0, 384)], DT.at[n, :, pl.ds(384, 384)], ts.at[0], tr.at[n], partner,
            device_id_type=MESH)

    def swap_h(n):
        return pltpu.make_async_remote_copy(
            HID.at[n, pl.ds(0, 192)], HID.at[n, pl.ds(192, 192)], ts.at[1], th.at[0], partner,
            device_id_type=MESH)

    def hidden(n):
        swap_gu(n).wait_recv()
        g = OWN[n, 0:192] + RCV[n, 0:192].astype(F32)
        u = OWN[n, 192:384] + RCV[n, 192:384].astype(F32)
        sg = jax.nn.sigmoid(g)
        gsg = g * sg
        HID[n, 0:192] = (gsg * u).astype(BF)
        OWN[n, 0:192] = u * sg * (1.0 + g * (1.0 - sg))
        OWN[n, 192:384] = gsg
        swap_h(n).start()

    def middle(n):
        swap_z(n).wait_recv()
        z = OWN[n, 384:576] + RCV[n, 384:576].astype(F32)
        d = jnp.concatenate([OWN[n, 0:192] * z, OWN[n, 192:384] * z], axis=0).astype(BF)
        DT[n, :, 0:384] = d.T
        swap_d(n).start()
        GROW[n] = jnp.broadcast_to(jnp.sum(HID[n, 0:192].astype(F32) * z, axis=0, keepdims=True), (8, 384))

    def grad_x(n, y):
        cols = pl.ds(pl.multiple_of(y * 512, 512), 512)
        XS[n, :, cols] = jnp.dot(DT[n], W[n, 0:768, cols], preferred_element_type=F32).astype(BF)

    def scatter(q, y):
        rows = pl.ds(pl.multiple_of(q * 48, 16), 48)
        cols = pl.ds(pl.multiple_of(y * 512, 512), 512)
        part = jnp.concatenate([XS[n, rows, cols] for n in range(4)], axis=0)
        r = jnp.dot(PT[q], part, preferred_element_type=F32).astype(BF)
        for b in range(2):
            for c in range(4):
                G[0, (2 * q + b) * 4 + y, c * 128:(c + 1) * 128, :] = (
                    r[b * 128:(b + 1) * 128, c * 128:(c + 1) * 128])

    def out_local(n, y):
        cols = pl.multiple_of(y * 1024 + core * 512, 512)
        return pltpu.make_async_copy(
            XS.at[n, pl.ds(0, 192), pl.ds(y * 512, 512)], gd.at[n, :, pl.ds(cols, 512)], ol.at[0])

    def out_remote(n, y):
        cols = pl.multiple_of(y * 1024 + core * 512, 512)
        return pltpu.make_async_remote_copy(
            XS.at[n, pl.ds(192, 192), pl.ds(y * 512, 512)], gd.at[n, :, pl.ds(cols, 512)],
            osnd.at[0], orcv.at[0], partner, device_id_type=MESH)

    def grad_down(n):
        h = HID[n]
        for y in range(4):
            cols = slice(y * 512, (y + 1) * 512)
            XS[n, :, cols] = jnp.dot(h, DY[n, :, cols], preferred_element_type=F32).astype(BF)
            out_local(n, y).start()
            out_remote(n, y).start()

    def gate_tokens():
        lane = lax.broadcasted_iota(jnp.int32, (8, 192), 1)
        row = lax.broadcasted_iota(jnp.int32, (8, 192), 0)
        own = (lane >= row * 48) & (lane < row * 48 + 48)
        for q in range(8):
            vals = jnp.concatenate([GROW[n, 0:1, q * 48:(q + 1) * 48] for n in range(4)], axis=1)
            a = jnp.where(own, vals, 0.0)
            gt = jnp.dot(a, PM[q].astype(F32), precision=lax.Precision.HIGHEST, preferred_element_type=F32)
            ids = pair_ids(q)
            r = jnp.zeros((8, 256), F32)
            for n in range(4):
                r = r + jnp.where(ids == first + float(n), gt[n:n + 1], 0.0)
            GS[2 * q] = r[:, 0:128]
            GS[2 * q + 1] = r[:, 128:256]

    def gate_one(i):
        e = (ex + i) % 16
        return pltpu.make_async_remote_copy(
            GS.at[e], GR.at[i], gs1.at[0], gr1.at[0], (dp, e), device_id_type=MESH)

    def gate_two(i):
        return pltpu.make_async_remote_copy(
            GT, GX.at[i], gs2.at[0], gr2.at[0], ((dp + i) % 8, ex), device_id_type=MESH)

    def member(p, k, i):
        return group(k, i) if p == 1 else group(i, k)

    def rslot(s, p, j):
        if s < 2:
            return slot(s, j)
        return slot(2, j % 4 if p == 1 else j // 4)

    def rhalf(s, p, j, way):
        a = ORDER[p][s]
        k = blk(shift(origin(s, p, j), a, 2))
        rows = half_rows(p, way)
        return pltpu.make_async_remote_copy(
            G.at[0, k, rows], G.at[1, BASE[s] + j, rows], sent.at[sent_sem(0, p, way)],
            fr.at[full_sem(0, p, way, rslot(s, p, j))], nbr[a][way], device_id_type=MESH)

    def rfull(s, p, j, way):
        a = ORDER[p][s]
        k = blk(shift(origin(s, p, j), a, 1 if way == 0 else 3))
        rows = part_rows(p)
        return pltpu.make_async_remote_copy(
            G.at[0, k, rows], G.at[1, 21 + (BASE[s] + j) * 2 + way, rows], sent.at[sent_sem(0, p, way)],
            fr.at[full_sem(1, p, way, rslot(s, p, j))], nbr[a][way], device_id_type=MESH)

    def add_half(s, p, j, way):
        k = blk(shift(origin(s, p, j), ORDER[p][s], 1 if way == 0 else 3))
        rows = half_rows(p, way)
        G[0, k, rows] = (G[0, k, rows].astype(F32) + G[1, BASE[s] + j, rows].astype(F32)).astype(BF)
        rfull(s, p, j, way).start()

    def add_full(s, p, j):
        k = blk(origin(s, p, j))
        rows = part_rows(p)
        f = 21 + (BASE[s] + j) * 2
        G[0, k, rows] = (G[0, k, rows].astype(F32) + (
            G[1, f, rows].astype(F32) + G[1, f + 1, rows].astype(F32))).astype(BF)

    def start2(p, k):
        def one(i):
            rhalf(2, p, member(p, k, i), 0).start()
            rhalf(2, p, member(p, k, i), 1).start()
        loop(0, 4, one)

    def mid2(p, k):
        for w in range(2):
            settle(G.at[1, pl.ds(0, 4), half_rows(p, w)], fr.at[full_sem(0, p, w, slot(2, k))])
            loop(0, 4, lambda i, w=w: add_half(2, p, member(p, k, i), w))

    def end2(p, k):
        for w in range(2):
            settle(G.at[1, pl.ds(0, 4), part_rows(p)], fr.at[full_sem(1, p, w, slot(2, k))])
        loop(0, 4, lambda i: add_full(2, p, member(p, k, i)))

    def start(s, p, j):
        for w in range(2):
            rhalf(s, p, j, w).start()

    def mid(s, p, j):
        for w in range(2):
            rhalf(s, p, j, w).wait_recv()
            add_half(s, p, j, w)

    def end(s, p, j):
        for w in range(2):
            rfull(s, p, j, w).wait_recv()
        add_full(s, p, j)

    far = (2, 3, 1, 0)
    for i in range(1, 16):
        meta_copy(i).start()
    ev0 = gather_events(0)
    ev1 = gather_events(1)
    ev0[0]()
    fetch_weights()
    ev0[1]()
    ev0[2]()
    ev0[3]()
    settle(META.at[pl.ds(0, 15)], mr.at[0])
    settle(META.at[pl.ds(0, 15)], ms.at[0])
    for e in ev0[4:7]:
        e()
    prepare()
    for e in ev0[7:10]:
        e()
    ev1[0]()
    for e in ev0[10:]:
        e()
    for e in ev1[1:4]:
        e()
    gather_rest(0)
    loop(0, 4, lambda q: select(0, q))
    ev1[4]()
    ev1[5]()
    loop(4, 8, lambda q: select(0, q))
    ev1[6]()
    ev1[7]()
    settle_weights()
    loop(0, 2, gate_up)
    ev1[8]()
    ev1[9]()
    loop(2, 4, gate_up)
    ev1[10]()
    loop(0, 2, hidden)
    ev1[11]()
    loop(2, 4, hidden)
    gather_rest(1)
    loop(0, 8, lambda q: select(1, q))
    all_sent(0)
    all_sent(1)
    for a in range(3):
        for n in nbr[a]:
            pl.semaphore_signal(ready, inc=1, device_id=n, device_id_type=MESH)
    loop(0, 4, down)
    loop(0, 4, middle)
    loop(0, 4, lambda n: swap_d(n).wait_recv())

    def columns(b):
        y = (pos[1] + b) % 4
        loop(0, 4, lambda n: grad_x(n, y))
        loop(0, 8, lambda q: scatter(q, y))

    columns(2)
    pl.semaphore_wait(ready, 6)
    start2(0, 2)
    start2(1, 2)
    for k in far:
        start2(2, k)
    columns(3)
    start2(0, 3)
    start2(1, 3)
    mid2(0, 2)
    mid2(1, 2)
    columns(1)
    start2(0, 1)
    start2(1, 1)
    mid2(0, 3)
    mid2(1, 3)
    mid2(2, 2)
    mid2(2, 3)
    columns(0)
    start2(0, 0)
    start2(1, 0)
    mid2(2, 1)
    mid2(2, 0)
    mid2(0, 1)
    mid2(1, 1)
    gate_tokens()
    for i in range(1, 16):
        gate_one(i).start()
    end2(0, 2)
    loop(0, 4, lambda a: start(1, 0, a))
    end2(1, 2)
    start(1, 1, 2)
    end2(2, 2)
    loop(0, 4, lambda a: start(1, 2, a))
    mid2(0, 0)
    mid2(1, 0)
    settle(HID.at[:, pl.ds(0, 192)], th.at[0])
    loop(0, 4, grad_down)
    end2(1, 3)
    start(1, 1, 3)
    end2(1, 1)
    start(1, 1, 1)
    mid(1, 1, 2)
    for p in (0, 2):
        end2(p, 3)
        end2(p, 1)
        loop(0, 4, lambda a, p=p: mid(1, p, (a + 2) % 4))
    end2(1, 0)
    start(1, 1, 0)
    odd(lambda a: mid(1, 1, a))
    end2(0, 0)
    end2(2, 0)
    mid(1, 1, 0)
    for p in range(3):
        end(1, p, 2)
        start(0, p, 0)
    settle(GR.at[pl.ds(0, 15)], gr1.at[0])
    acc = GS[ex]
    for i in range(1, 16):
        acc = acc + GR[i]
    GT[...] = acc
    for i in range(1, 8):
        gate_two(i).start()
    for p in range(3):
        odd(lambda a, p=p: end(1, p, a))
        mid(0, p, 0)
    for p in range(3):
        end(1, p, 0)
    settle(GX.at[pl.ds(0, 7)], gr2.at[0])
    acc = GT[...]
    for i in range(1, 8):
        acc = acc + GX[i]
    gates[...] = acc / gpt[...]
    for p in range(3):
        end(0, p, 0)
    for c in range(4):
        dxo[:, c * 128:(c + 1) * 128] = G[0, me, c * 128:(c + 1) * 128, :]
    all_sent(0)
    settle(GR.at[pl.ds(0, 15)], gs1.at[0])
    settle(GX.at[pl.ds(0, 7)], gs2.at[0])
    settle(SND, es.at[0])
    settle(DT.at[:, :, pl.ds(0, 384)], ts.at[0])
    settle(HID.at[:, pl.ds(0, 192)], ts.at[1])
    for sem in (ol, osnd, orcv):
        settle(XS.at[:, pl.ds(0, 192)], sem.at[0])


def on_device(
    tokens, grad_out, expert_ids, gate_probs, seq_ids, log_ratio, advantages, w_gate, w_up, w_down
):
    vmem = pl.BlockSpec(memory_space=pltpu.VMEM)
    hbm = pl.BlockSpec(memory_space=pl.ANY)
    dma = lambda n: pltpu.SemaphoreType.DMA((n,))
    dx, gates, gd = pl.pallas_call(
        step_kernel,
        out_shape=(
            jax.ShapeDtypeStruct((128, 512), BF),
            jax.ShapeDtypeStruct((8, 128), F32),
            jax.ShapeDtypeStruct((4, 192, 4096), BF),
        ),
        in_specs=[pl.BlockSpec(memory_space=pltpu.SMEM)] + [vmem] * 6 + [hbm] * 3,
        out_specs=(vmem, vmem, hbm),
        scratch_shapes=[
            pltpu.VMEM((2, 64, 512, 128), BF),
            pltpu.VMEM((4, 384, 2048), BF),
            pltpu.VMEM((4, 384, 2048), BF),
            pltpu.VMEM((4, 1152, 2048), BF),
            pltpu.VMEM((4, 576, 384), F32),
            pltpu.VMEM((4, 576, 384), BF),
            pltpu.VMEM((4, 576, 384), BF),
            pltpu.VMEM((4, 384, 768), BF),
            pltpu.VMEM((4, 384, 384), BF),
            pltpu.VMEM((8, 192, 256), BF),
            pltpu.VMEM((8, 256, 192), BF),
            pltpu.VMEM((8, 192, 128), F32),
            pltpu.VMEM((16, 24, 128), F32),
            pltpu.VMEM((4, 8, 384), F32),
            pltpu.VMEM((16, 8, 128), F32),
            pltpu.VMEM((16, 8, 128), F32),
            pltpu.VMEM((8, 128), F32),
            pltpu.VMEM((8, 8, 128), F32),
            dma(2), dma(12), dma(108), dma(72), dma(1), dma(1), dma(1), dma(1), dma(1),
            dma(1), dma(8), dma(2), dma(4), dma(1), dma(1), dma(1), dma(1), dma(1), dma(1), dma(1), dma(1),
            pltpu.SemaphoreType.REGULAR,
        ],
        compiler_params=pltpu.CompilerParams(
            collective_id=0, has_side_effects=True, vmem_limit_bytes=67043328),
        name="expert_step",
    )(
        advantages, tokens, grad_out, expert_ids.T, gate_probs.T, seq_ids.reshape(1, -1), log_ratio.reshape(1, -1),
        w_gate, w_up, w_down)
    return dx, gates.T, gd


def solution(mesh):
    return jax.shard_map(
        on_device,
        mesh=mesh,
        in_specs=(
            P("expert", "dp"),
            P("expert", "dp"),
            P("expert", None),
            P("expert", None),
            P("expert"),
            P("expert"),
            P(),
            P("expert", "dp", None),
            P("expert", "dp", None),
            P("expert", "dp", None),
        ),
        out_specs=(P("expert", "dp"), P("expert", None), P("expert", "dp", None)),
        check_vma=False,
    )
```

```python
import jax
import jax.numpy as jnp
from jax import lax
from jax.experimental import pallas as pl
from jax.experimental.pallas import tpu as pltpu
from jax.sharding import PartitionSpec as P

SEQS = 8
TOP = 8
CAP = 24
clip_low = 0.9
clip_high = 1.1

MESH = pl.DeviceIdType.MESH
BF = jnp.bfloat16
F32 = jnp.float32
PARTS = (
    ((0, 176, 96), (176, 176, 80), (352, 160, 80)),
    ((0, 176, 80), (176, 160, 80), (336, 176, 96)),
)
ORDER = ((0, 1, 2), (1, 2, 0), (2, 0, 1))
BASE = (0, 1, 5)
COUNT = (1, 4, 16)
NT = (((1,), (1,)), ((), ()))
TN = (((0,), (0,)), ((), ()))


def group(a, b):
    return b * 4 + a


def step_kernel(
    adv, tok, gout, idt, gpt, seq, ratio, wg, wu, wd,
    dxo, gates, gd,
    G, XS, DY, W, OWN, SND, RCV, DT, HID, PM, PT, CC, META, GROW, GS, GR, GT, GX,
    locsem, sent, fr, hr, wl, ws, wr, ms, mr,
    es, er, ts, tr, th, gs1, gr1, gs2, gr2, ol, osnd, orcv, ready,
):
    dp = lax.axis_index("dp")
    ex = lax.axis_index("expert")
    pos = [ex % 4, dp // 2, ex // 4]
    core = dp % 2

    def dev(q, c):
        return (q[1] * 2 + c, q[2] * 4 + q[0])

    def shift(q, a, n):
        q = list(q)
        q[a] = (q[a] + n) % 4
        return q

    def blk(q):
        return (q[2] * 4 + q[0]) * 4 + q[1]

    nbr = [(dev(shift(pos, a, 1), core), dev(shift(pos, a, 3), core)) for a in range(3)]
    partner = (pos[1] * 2 + 1 - core, ex)
    me = blk(pos)
    bar = pltpu.get_barrier_semaphore()
    for i in range(1, 16):
        pl.semaphore_signal(bar, inc=1, device_id=(dp, (ex + i) % 16), device_id_type=MESH)
    for i in range(1, 8):
        pl.semaphore_signal(bar, inc=1, device_id=((dp + i) % 8, ex), device_id_type=MESH)

    def settle(ref, sem):
        pltpu.make_async_copy(ref, ref, sem).wait()

    for c in range(4):
        for w, src in enumerate((tok, gout)):
            pltpu.make_async_copy(
                src.at[:, pl.ds(c * 128, 128)], G.at[w, me, pl.ds(c * 128, 128)], locsem.at[w]).start()
    META[ex, 0:8, :] = idt[...].astype(F32)
    META[ex, 8:16, :] = gpt[...]
    META[ex, 16:17, :] = seq[...].astype(F32)
    META[ex, 17:18, :] = ratio[...]

    def fetch_weights():
        for k, (src, r0, r1) in enumerate(((wg, 0, 384), (wu, 192, 576), (wd, 768, 960))):
            for y in range(4):
                mine = pl.multiple_of(y * 1024 + core * 512, 512)
                theirs = pl.multiple_of(y * 1024 + (1 - core) * 512, 512)
                pltpu.make_async_copy(
                    src.at[:, :, pl.ds(mine, 512)], W.at[:, pl.ds(r0, 192), pl.ds(y * 512, 512)], wl.at[0]).start()
                pltpu.make_async_remote_copy(
                    src.at[:, :, pl.ds(theirs, 512)], W.at[:, pl.ds(r1, 192), pl.ds(y * 512, 512)],
                    ws.at[0], wr.at[0], partner, device_id_type=MESH).start()

    def settle_weights():
        for sem in (wl, ws, wr):
            settle(W.at[:, pl.ds(0, 576)], sem.at[0])

    pl.semaphore_wait(bar, 22)
    for w in range(2):
        settle(G.at[w, me], locsem.at[w])

    def origin(s, p, j):
        q = list(pos)
        o = ORDER[p]
        if s >= 1:
            q = shift(q, o[0], j % 4)
        if s == 2:
            q = shift(q, o[1], j // 4)
        return q

    def slot(s, k):
        return (0, 1, 5)[s] + k

    def full_sem(v, p, way, k):
        return ((v * 3 + p) * 2 + way) * 10 + k

    def half_sem(v, p, way, k):
        return ((v * 3 + p) * 2 + way) * 6 + k

    def sent_sem(v, p, way):
        return (v * 3 + p) * 2 + way

    def half_rows(p, way, v=0):
        r0, n, h = PARTS[v][p]
        return pl.ds(r0, h) if way == 0 else pl.ds(r0 + h, n - h)

    def half_count(v, p, way):
        return PARTS[v][p][2] if way == 0 else PARTS[v][p][1] - PARTS[v][p][2]

    def part_rows(p, v=0):
        return pl.ds(PARTS[v][p][0], PARTS[v][p][1])

    def full(v, s, p, j, way):
        ref = G.at[v, blk(origin(s, p, j)), part_rows(p, v)]
        k = slot(s, j // 4 if s == 2 else j)
        return pltpu.make_async_remote_copy(
            ref, ref, sent.at[sent_sem(v, p, way)], fr.at[full_sem(v, p, way, k)], nbr[ORDER[p][s]][way],
            device_id_type=MESH)

    def half(v, s, p, j, way):
        a = ORDER[p][s]
        b = blk(shift(origin(s, p, j), a, 3 if way == 0 else 1))
        ref = G.at[v, b, half_rows(p, way, v)]
        k = 5 if s == 2 else slot(s, j)
        return pltpu.make_async_remote_copy(
            ref, ref, sent.at[sent_sem(v, p, way)], hr.at[half_sem(v, p, way, k)], nbr[a][way],
            device_id_type=MESH)

    def each(f):
        for p in range(3):
            for way in range(2):
                f(p, way)

    def odd(f):
        def body(i, c):
            f(1 + 2 * i)
            return c
        lax.fori_loop(0, 2, body, 0)

    def loop(lo, hi, f):
        def body(i, c):
            f(i)
            return c
        lax.fori_loop(lo, hi, body, 0)

    def send(v, s, j):
        each(lambda p, w: full(v, s, p, j, w).start())

    def hop(v, s, j):
        def one(p, w):
            full(v, s, p, j, w).wait_recv()
            half(v, s, p, j, w).start()
        each(one)

    def hop_bundle(v, b):
        for p in range(3):
            for w in range(2):
                settle(G.at[v, pl.ds(0, 4), part_rows(p, v)], fr.at[full_sem(v, p, w, slot(2, b))])
                loop(0, 4, lambda a, p=p, w=w: half(v, 2, p, group(a, b), w).start())

    def last(v, s, j):
        each(lambda p, w: half(v, s, p, j, w).wait_recv())

    def gather_events(v):
        ev = []
        ev.append(lambda: (send(v, 0, 0), send(v, 1, 0), send(v, 2, 0)))
        ev.append(lambda: (hop(v, 0, 0), odd(lambda a: send(v, 1, a)), odd(lambda a: send(v, 2, group(a, 0)))))
        ev.append(lambda: (hop(v, 1, 0), odd(lambda b: send(v, 2, group(0, b)))))
        ev.append(lambda: (last(v, 0, 0), send(v, 1, 2), send(v, 2, group(2, 0))))
        ev.append(lambda: odd(lambda a: (hop(v, 1, a), odd(lambda b: send(v, 2, group(a, b))))))
        ev.append(lambda: (last(v, 1, 0), send(v, 2, group(0, 2))))
        ev.append(lambda: hop_bundle(v, 0))
        ev.append(lambda: (hop(v, 1, 2), odd(lambda b: send(v, 2, group(2, b)))))
        ev.append(lambda: odd(lambda a: (last(v, 1, a), send(v, 2, group(a, 2)))))
        ev.append(lambda: (last(v, 1, 2), send(v, 2, group(2, 2))))
        ev.append(lambda: odd(lambda b: hop_bundle(v, b)))
        ev.append(lambda: hop_bundle(v, 2))
        return ev

    def gather_rest(v):
        def one(p, w):
            settle(G.at[v, pl.ds(0, 16), pl.ds(0, half_count(v, p, w))], hr.at[half_sem(v, p, w, 5)])
        each(one)

    def all_sent(v):
        def one(p, w):
            settle(G.at[v, pl.ds(0, 21), pl.ds(0, PARTS[v][p][1] + half_count(v, p, w))], sent.at[sent_sem(v, p, w)])
        each(one)

    def meta_copy(i):
        return pltpu.make_async_remote_copy(
            META.at[ex], META.at[ex], ms.at[0], mr.at[0], (dp, (ex + i) % 16), device_id_type=MESH)

    first = (ex * 4).astype(F32)

    def pair_ids(q):
        return jnp.concatenate([META[2 * q, 0:8], META[2 * q + 1, 0:8]], axis=1)

    def prepare():
        sid = META[:, 16, :]
        lr = META[:, 17, :]
        tw = jnp.zeros((16, 128), F32)
        for s in range(SEQS):
            hit = (sid == float(s)).astype(F32)
            total = jnp.sum(jnp.sum(hit * lr, axis=1, keepdims=True), axis=0, keepdims=True)
            count = jnp.sum(jnp.sum(hit, axis=1, keepdims=True), axis=0, keepdims=True)
            wt = adv[s] * jnp.clip(jnp.exp(total / count), clip_low, clip_high)
            tw = tw + hit * wt
        r = lax.broadcasted_iota(jnp.int32, (256, 256), 0)
        t = lax.broadcasted_iota(jnp.int32, (256, 256), 1)
        earlier = ((r < t) & ((r >= 128) == (t >= 128))).astype(F32).astype(BF)
        row = lax.broadcasted_iota(jnp.int32, (2 * CAP, 256), 0)
        lane = lax.broadcasted_iota(jnp.int32, (2 * CAP, 256), 1)
        second = row >= CAP
        same = second == (lane >= 128)
        slot = (row - jnp.where(second, CAP, 0)).astype(F32)
        for q in range(8):
            ids = pair_ids(q)
            gp = jnp.concatenate([META[2 * q, 8:16], META[2 * q + 1, 8:16]], axis=1)
            twq = jnp.concatenate([tw[2 * q:2 * q + 1], tw[2 * q + 1:2 * q + 2]], axis=1)
            hot, cw = [], []
            for n in range(4):
                hit = (ids == first + float(n)).astype(F32)
                hot.append(jnp.sum(hit, axis=0, keepdims=True))
                cw.append(jnp.sum(hit * gp, axis=0, keepdims=True) * twq)
            hots = jnp.concatenate(hot + hot, axis=0)
            rank = jnp.dot(hots.astype(BF), earlier, preferred_element_type=F32)
            for n in range(4):
                sel = same & (rank[n:n + 1] == slot) & (hot[n] > 0.5)
                pick = sel.astype(F32)
                PM[q, n * 48:(n + 1) * 48, :] = pick.astype(BF)
                cc = jnp.sum(pick * cw[n], axis=1, keepdims=True)
                CC[q, n * 48:(n + 1) * 48, :] = jnp.broadcast_to(cc, (48, 128))
            PT[q] = PM[q].T

    def select(v, q):
        dst = XS if v == 0 else DY
        rows = pl.ds(pl.multiple_of(q * 48, 16), 48)
        pm = PM[q]
        for y in range(4):
            xp = jnp.concatenate([
                jnp.concatenate([G[v, (2 * q + b) * 4 + y, c * 128:(c + 1) * 128, :] for c in range(4)], axis=1)
                for b in range(2)], axis=0)
            r = jnp.dot(pm, xp, preferred_element_type=F32)
            if v == 1:
                r = r * CC[q, :, 0:1]
            r = r.astype(BF)
            for n in range(4):
                dst[n, rows, y * 512:(y + 1) * 512] = r[n * 48:(n + 1) * 48]

    def swap_gu(n):
        return pltpu.make_async_remote_copy(
            SND.at[n, pl.ds(0, 384)], RCV.at[n, pl.ds(0, 384)], es.at[0], er.at[n], partner, device_id_type=MESH)

    def swap_z(n):
        return pltpu.make_async_remote_copy(
            SND.at[n, pl.ds(384, 192)], RCV.at[n, pl.ds(384, 192)], es.at[0], er.at[4 + n], partner,
            device_id_type=MESH)

    def gate_up(n):
        x = XS[n]
        OWN[n, 0:384] = lax.dot_general(W[n, 0:384], x, NT, preferred_element_type=F32)
        SND[n, 0:384] = lax.dot_general(W[n, 384:768], x, NT, preferred_element_type=F32).astype(BF)
        swap_gu(n).start()

    def down(n):
        z = lax.dot_general(W[n, 768:1152], DY[n], NT, preferred_element_type=F32)
        OWN[n, 384:576] = z[0:192]
        SND[n, 384:576] = z[192:384].astype(BF)
        swap_z(n).start()

    def swap_d(n):
        return pltpu.make_async_remote_copy(
            DT.at[n, :, pl.ds(0, 384)], DT.at[n, :, pl.ds(384, 384)], ts.at[0], tr.at[n], partner,
            device_id_type=MESH)

    def swap_h(n):
        return pltpu.make_async_remote_copy(
            HID.at[n, pl.ds(0, 192)], HID.at[n, pl.ds(192, 192)], ts.at[1], th.at[0], partner,
            device_id_type=MESH)

    def hidden(n):
        swap_gu(n).wait_recv()
        g = OWN[n, 0:192] + RCV[n, 0:192].astype(F32)
        u = OWN[n, 192:384] + RCV[n, 192:384].astype(F32)
        sg = jax.nn.sigmoid(g)
        gsg = g * sg
        HID[n, 0:192] = (gsg * u).astype(BF)
        OWN[n, 0:192] = u * sg * (1.0 + g * (1.0 - sg))
        OWN[n, 192:384] = gsg
        swap_h(n).start()

    def middle(n):
        swap_z(n).wait_recv()
        z = OWN[n, 384:576] + RCV[n, 384:576].astype(F32)
        d = jnp.concatenate([OWN[n, 0:192] * z, OWN[n, 192:384] * z], axis=0).astype(BF)
        DT[n, :, 0:384] = d.T
        swap_d(n).start()
        GROW[n] = jnp.broadcast_to(jnp.sum(HID[n, 0:192].astype(F32) * z, axis=0, keepdims=True), (8, 384))

    def grad_x(n, y):
        cols = pl.ds(pl.multiple_of(y * 512, 512), 512)
        XS[n, :, cols] = jnp.dot(DT[n], W[n, 0:768, cols], preferred_element_type=F32).astype(BF)

    def scatter(q, y):
        rows = pl.ds(pl.multiple_of(q * 48, 16), 48)
        cols = pl.ds(pl.multiple_of(y * 512, 512), 512)
        part = jnp.concatenate([XS[n, rows, cols] for n in range(4)], axis=0)
        r = jnp.dot(PT[q], part, preferred_element_type=F32).astype(BF)
        for b in range(2):
            for c in range(4):
                G[0, (2 * q + b) * 4 + y, c * 128:(c + 1) * 128, :] = (
                    r[b * 128:(b + 1) * 128, c * 128:(c + 1) * 128])

    def out_local(n, y):
        cols = pl.multiple_of(y * 1024 + core * 512, 512)
        return pltpu.make_async_copy(
            XS.at[n, pl.ds(0, 192), pl.ds(y * 512, 512)], gd.at[n, :, pl.ds(cols, 512)], ol.at[0])

    def out_remote(n, y):
        cols = pl.multiple_of(y * 1024 + core * 512, 512)
        return pltpu.make_async_remote_copy(
            XS.at[n, pl.ds(192, 192), pl.ds(y * 512, 512)], gd.at[n, :, pl.ds(cols, 512)],
            osnd.at[0], orcv.at[0], partner, device_id_type=MESH)

    def grad_down(n):
        h = HID[n]
        for y in range(4):
            cols = slice(y * 512, (y + 1) * 512)
            XS[n, :, cols] = jnp.dot(h, DY[n, :, cols], preferred_element_type=F32).astype(BF)
            out_local(n, y).start()
            out_remote(n, y).start()

    def gate_tokens():
        lane = lax.broadcasted_iota(jnp.int32, (8, 192), 1)
        row = lax.broadcasted_iota(jnp.int32, (8, 192), 0)
        own = (lane >= row * 48) & (lane < row * 48 + 48)
        for q in range(8):
            vals = jnp.concatenate([GROW[n, 0:1, q * 48:(q + 1) * 48] for n in range(4)], axis=1)
            a = jnp.where(own, vals, 0.0)
            gt = jnp.dot(a, PM[q].astype(F32), precision=lax.Precision.HIGHEST, preferred_element_type=F32)
            ids = pair_ids(q)
            r = jnp.zeros((8, 256), F32)
            for n in range(4):
                r = r + jnp.where(ids == first + float(n), gt[n:n + 1], 0.0)
            GS[2 * q] = r[:, 0:128]
            GS[2 * q + 1] = r[:, 128:256]

    def gate_one(i):
        e = (ex + i) % 16
        return pltpu.make_async_remote_copy(
            GS.at[e], GR.at[i], gs1.at[0], gr1.at[0], (dp, e), device_id_type=MESH)

    def gate_two(i):
        return pltpu.make_async_remote_copy(
            GT, GX.at[i], gs2.at[0], gr2.at[0], ((dp + i) % 8, ex), device_id_type=MESH)

    def member(p, k, i):
        return group(k, i) if p == 1 else group(i, k)

    def rhalf(s, p, j, way, k=0):
        a = ORDER[p][s]
        b = blk(shift(origin(s, p, j), a, 2))
        rows = half_rows(p, way)
        sem = slot(2, k) if s == 2 else slot(s, j)
        return pltpu.make_async_remote_copy(
            G.at[0, b, rows], G.at[1, BASE[s] + j, rows], sent.at[sent_sem(0, p, way)],
            fr.at[full_sem(0, p, way, sem)], nbr[a][way], device_id_type=MESH)

    def rfull(s, p, j, way, k=0):
        a = ORDER[p][s]
        b = blk(shift(origin(s, p, j), a, 1 if way == 0 else 3))
        rows = part_rows(p)
        sem = slot(2, k) if s == 2 else slot(s, j)
        return pltpu.make_async_remote_copy(
            G.at[0, b, rows], G.at[1, 21 + (BASE[s] + j) * 2 + way, rows], sent.at[sent_sem(0, p, way)],
            fr.at[full_sem(1, p, way, sem)], nbr[a][way], device_id_type=MESH)

    def add_half(s, p, j, way, f=0):
        k = blk(shift(origin(s, p, j), ORDER[p][s], 1 if way == 0 else 3))
        rows = half_rows(p, way)
        G[0, k, rows] = (G[0, k, rows].astype(F32) + G[1, BASE[s] + j, rows].astype(F32)).astype(BF)
        rfull(s, p, j, way, f).start()

    def add_full(s, p, j):
        k = blk(origin(s, p, j))
        rows = part_rows(p)
        f = 21 + (BASE[s] + j) * 2
        G[0, k, rows] = (G[0, k, rows].astype(F32) + (
            G[1, f, rows].astype(F32) + G[1, f + 1, rows].astype(F32))).astype(BF)

    def start2(p, k):
        def one(i):
            rhalf(2, p, member(p, k, i), 0, k).start()
            rhalf(2, p, member(p, k, i), 1, k).start()
        loop(0, 4, one)

    def halves_in(p, k):
        for w in range(2):
            settle(G.at[1, pl.ds(0, 4), half_rows(p, w)], fr.at[full_sem(0, p, w, slot(2, k))])

    def pass_on(p, k, i, f):
        for w in range(2):
            add_half(2, p, member(p, k, i), w, f)

    def mid2(p, step):
        if step == 0:
            halves_in(p, 2)
            loop(0, 4, lambda i: pass_on(p, 2, (i + 2) % 4, 0))
        elif step == 1:
            halves_in(p, 3)
            loop(1, 4, lambda i: pass_on(p, 3, i, 1))
        elif step == 2:
            halves_in(p, 1)
            loop(1, 4, lambda i: pass_on(p, 1, i, 1))
        elif step == 3:
            halves_in(p, 0)
            pass_on(p, 0, 2, 2)
        elif step == 4:
            odd(lambda k: pass_on(p, k, 0, 3))
            odd(lambda i: pass_on(p, 0, i, 3))
        else:
            pass_on(p, 0, 0, 4)

    def end2(p, f):
        n = (4, 6, 1, 4, 1)[f]
        for w in range(2):
            settle(G.at[1, pl.ds(0, n), part_rows(p)], fr.at[full_sem(1, p, w, slot(2, f))])
        take = lambda k, i: add_full(2, p, member(p, k, i))
        if f == 0:
            loop(0, 4, lambda i: take(2, i))
        elif f == 1:
            odd(lambda k: loop(1, 4, lambda i: take(k, i)))
        elif f == 2:
            take(0, 2)
        elif f == 3:
            odd(lambda k: take(k, 0))
            odd(lambda i: take(0, i))
        else:
            take(0, 0)

    def start(s, p, j):
        for w in range(2):
            rhalf(s, p, j, w).start()

    def mid(s, p, j):
        for w in range(2):
            rhalf(s, p, j, w).wait_recv()
            add_half(s, p, j, w)

    def end(s, p, j):
        for w in range(2):
            rfull(s, p, j, w).wait_recv()
        add_full(s, p, j)

    far = (2, 3, 1, 0)
    for i in range(1, 16):
        meta_copy(i).start()
    ev0 = gather_events(0)
    ev1 = gather_events(1)
    ev0[0]()
    fetch_weights()
    ev0[1]()
    ev0[2]()
    ev0[3]()
    settle(META.at[pl.ds(0, 15)], mr.at[0])
    settle(META.at[pl.ds(0, 15)], ms.at[0])
    for e in ev0[4:7]:
        e()
    prepare()
    for e in ev0[7:10]:
        e()
    ev1[0]()
    for e in ev0[10:]:
        e()
    for e in ev1[1:4]:
        e()
    gather_rest(0)
    loop(0, 4, lambda q: select(0, q))
    ev1[4]()
    ev1[5]()
    loop(4, 8, lambda q: select(0, q))
    ev1[6]()
    ev1[7]()
    settle_weights()
    loop(0, 2, gate_up)
    ev1[8]()
    ev1[9]()
    loop(2, 4, gate_up)
    ev1[10]()
    loop(0, 2, hidden)
    ev1[11]()
    loop(2, 4, hidden)
    gather_rest(1)
    loop(0, 8, lambda q: select(1, q))
    all_sent(0)
    all_sent(1)
    for a in range(3):
        for n in nbr[a]:
            pl.semaphore_signal(ready, inc=1, device_id=n, device_id_type=MESH)
    loop(0, 4, down)
    loop(0, 4, middle)
    loop(0, 4, lambda n: swap_d(n).wait_recv())

    def columns(b):
        y = (pos[1] + b) % 4
        loop(0, 4, lambda n: grad_x(n, y))
        loop(0, 8, lambda q: scatter(q, y))

    columns(2)
    pl.semaphore_wait(ready, 6)
    start2(0, 2)
    start2(1, 2)
    for k in far:
        start2(2, k)
    columns(3)
    start2(0, 3)
    start2(1, 3)
    columns(1)
    start2(0, 1)
    start2(1, 1)
    for p in range(3):
        mid2(p, 0)
    columns(0)
    start2(0, 0)
    start2(1, 0)
    for p in range(3):
        end2(p, 0)
        if p == 1:
            start(1, 1, 2)
        else:
            loop(0, 4, lambda a, p=p: start(1, p, (a + 2) % 4))
    for p in range(3):
        mid2(p, 1)
    gate_tokens()
    for i in range(1, 16):
        gate_one(i).start()
    for p in range(3):
        mid2(p, 2)
    mid(1, 1, 2)
    for p in range(3):
        mid2(p, 3)
    settle(HID.at[:, pl.ds(0, 192)], th.at[0])
    loop(0, 4, grad_down)
    for p in range(3):
        end2(p, 1)
        if p == 1:
            odd(lambda a: start(1, 1, a))
        else:
            loop(1, 4, lambda a, p=p: mid(1, p, a))
    for p in range(3):
        mid2(p, 4)
    settle(GR.at[pl.ds(0, 15)], gr1.at[0])
    acc = GS[ex]
    for i in range(1, 16):
        acc = acc + GR[i]
    GT[...] = acc
    for i in range(1, 8):
        gate_two(i).start()
    for p in range(3):
        end2(p, 2)
        if p == 1:
            start(1, 1, 0)
        end(1, p, 2)
        start(0, p, 0)
    for p in range(3):
        mid2(p, 5)
    odd(lambda a: mid(1, 1, a))
    for p in range(3):
        end2(p, 3)
        mid(1, p, 0)
        odd(lambda a, p=p: end(1, p, a))
        mid(0, p, 0)
    for p in range(3):
        end2(p, 4)
        end(1, p, 0)
    settle(GX.at[pl.ds(0, 7)], gr2.at[0])
    acc = GT[...]
    for i in range(1, 8):
        acc = acc + GX[i]
    gates[...] = acc / gpt[...]
    for p in range(3):
        end(0, p, 0)
    for c in range(4):
        dxo[:, c * 128:(c + 1) * 128] = G[0, me, c * 128:(c + 1) * 128, :]
    all_sent(0)
    settle(GR.at[pl.ds(0, 15)], gs1.at[0])
    settle(GX.at[pl.ds(0, 7)], gs2.at[0])
    settle(SND, es.at[0])
    settle(DT.at[:, :, pl.ds(0, 384)], ts.at[0])
    settle(HID.at[:, pl.ds(0, 192)], ts.at[1])
    for sem in (ol, osnd, orcv):
        settle(XS.at[:, pl.ds(0, 192)], sem.at[0])


def store_kernel(gd, dx, gt, gdo, dxo, gto, B, DB, GB, arrive, leave):
    pairs = [(gd.at[i // 4, pl.ds(i % 4 * 48, 48)], B.at[i], gdo.at[i // 4, pl.ds(i % 4 * 48, 48)]) for i in range(16)]
    pairs += [(dx, DB, dxo), (gt, GB, gto)]
    for i, (src, buf, dst) in enumerate(pairs):
        pltpu.make_async_copy(src, buf, arrive.at[i]).start()
    for i, (src, buf, dst) in enumerate(pairs):
        pltpu.make_async_copy(src, buf, arrive.at[i]).wait()
        pltpu.make_async_copy(buf, dst, leave.at[i]).start()
    for i, (src, buf, dst) in enumerate(pairs):
        pltpu.make_async_copy(buf, dst, leave.at[i]).wait()


def on_device(
    tokens, grad_out, expert_ids, gate_probs, seq_ids, log_ratio, advantages, w_gate, w_up, w_down
):
    vmem = pl.BlockSpec(memory_space=pltpu.VMEM)
    hbm = pl.BlockSpec(memory_space=pl.ANY)
    dma = lambda n: pltpu.SemaphoreType.DMA((n,))
    dx, gates, gd = pl.pallas_call(
        step_kernel,
        out_shape=(
            jax.ShapeDtypeStruct((128, 512), BF),
            jax.ShapeDtypeStruct((8, 128), F32),
            jax.ShapeDtypeStruct((4, 192, 4096), BF),
        ),
        in_specs=[pl.BlockSpec(memory_space=pltpu.SMEM)] + [vmem] * 6 + [hbm] * 3,
        out_specs=(vmem, vmem, hbm),
        scratch_shapes=[
            pltpu.VMEM((2, 64, 512, 128), BF),
            pltpu.VMEM((4, 384, 2048), BF),
            pltpu.VMEM((4, 384, 2048), BF),
            pltpu.VMEM((4, 1152, 2048), BF),
            pltpu.VMEM((4, 576, 384), F32),
            pltpu.VMEM((4, 576, 384), BF),
            pltpu.VMEM((4, 576, 384), BF),
            pltpu.VMEM((4, 384, 768), BF),
            pltpu.VMEM((4, 384, 384), BF),
            pltpu.VMEM((8, 192, 256), BF),
            pltpu.VMEM((8, 256, 192), BF),
            pltpu.VMEM((8, 192, 128), F32),
            pltpu.VMEM((16, 24, 128), F32),
            pltpu.VMEM((4, 8, 384), F32),
            pltpu.VMEM((16, 8, 128), F32),
            pltpu.VMEM((16, 8, 128), F32),
            pltpu.VMEM((8, 128), F32),
            pltpu.VMEM((8, 8, 128), F32),
            dma(2), dma(12), dma(120), dma(72), dma(1), dma(1), dma(1), dma(1), dma(1),
            dma(1), dma(8), dma(2), dma(4), dma(1), dma(1), dma(1), dma(1), dma(1), dma(1), dma(1), dma(1),
            pltpu.SemaphoreType.REGULAR,
        ],
        compiler_params=pltpu.CompilerParams(
            collective_id=0, has_side_effects=True, vmem_limit_bytes=67043328),
        name="expert_step",
    )(
        advantages, tokens, grad_out, expert_ids.T, gate_probs.T, seq_ids.reshape(1, -1), log_ratio.reshape(1, -1),
        w_gate, w_up, w_down)
    gd, dx, gates = pl.pallas_call(
        store_kernel,
        out_shape=(
            jax.ShapeDtypeStruct((4, 192, 4096), BF),
            jax.ShapeDtypeStruct((128, 512), BF),
            jax.ShapeDtypeStruct((8, 128), F32),
        ),
        in_specs=[hbm] * 3,
        out_specs=(hbm,) * 3,
        scratch_shapes=[
            pltpu.VMEM((16, 48, 4096), BF), pltpu.VMEM((128, 512), BF), pltpu.VMEM((8, 128), F32), dma(18), dma(18),
        ],
        name="store_results",
    )(gd, dx, gates)
    return dx, gates.T, gd


def solution(mesh):
    return jax.shard_map(
        on_device,
        mesh=mesh,
        in_specs=(
            P("expert", "dp"),
            P("expert", "dp"),
            P("expert", None),
            P("expert", None),
            P("expert"),
            P("expert"),
            P(),
            P("expert", "dp", None),
            P("expert", "dp", None),
            P("expert", "dp", None),
        ),
        out_specs=(P("expert", "dp"), P("expert", None), P("expert", "dp", None)),
        check_vma=False,
    )
```

```python
import jax
import jax.numpy as jnp
from jax import lax
from jax.experimental import pallas as pl
from jax.experimental.pallas import tpu as pltpu
from jax.sharding import PartitionSpec as P

SEQS = 8
TOP = 8
CAP = 24
clip_low = 0.9
clip_high = 1.1

MESH = pl.DeviceIdType.MESH
BF = jnp.bfloat16
F32 = jnp.float32
PARTS = (
    ((0, 176, 96), (176, 176, 80), (352, 160, 80)),
    ((0, 176, 80), (176, 160, 80), (336, 176, 96)),
)
ORDER = ((0, 1, 2), (1, 2, 0), (2, 0, 1))
BASE = (0, 1, 5)
COUNT = (1, 4, 16)
NT = (((1,), (1,)), ((), ()))
TN = (((0,), (0,)), ((), ()))


def group(a, b):
    return b * 4 + a


def step_kernel(
    adv, tok, gout, idt, gpt, seq, ratio, wg, wu, wd,
    dxo, gates, gd,
    G, XS, DY, W, OWN, SND, RCV, DT, HID, PM, PT, CC, META, GROW, GS, GR, GT, GX,
    locsem, sent, fr, hr, wl, ws, wr, ms, mr,
    es, er, ts, tr, th, gs1, gr1, gs2, gr2, ol, osnd, orcv, ready,
):
    dp = lax.axis_index("dp")
    ex = lax.axis_index("expert")
    pos = [ex % 4, dp // 2, ex // 4]
    core = dp % 2

    def dev(q, c):
        return (q[1] * 2 + c, q[2] * 4 + q[0])

    def shift(q, a, n):
        q = list(q)
        q[a] = (q[a] + n) % 4
        return q

    def blk(q):
        return (q[2] * 4 + q[0]) * 4 + q[1]

    nbr = [(dev(shift(pos, a, 1), core), dev(shift(pos, a, 3), core)) for a in range(3)]
    partner = (pos[1] * 2 + 1 - core, ex)
    me = blk(pos)
    bar = pltpu.get_barrier_semaphore()
    for i in range(1, 16):
        pl.semaphore_signal(bar, inc=1, device_id=(dp, (ex + i) % 16), device_id_type=MESH)
    for i in range(1, 8):
        pl.semaphore_signal(bar, inc=1, device_id=((dp + i) % 8, ex), device_id_type=MESH)

    def settle(ref, sem):
        pltpu.make_async_copy(ref, ref, sem).wait()

    for c in range(4):
        for w, src in enumerate((tok, gout)):
            pltpu.make_async_copy(
                src.at[:, pl.ds(c * 128, 128)], G.at[w, me, pl.ds(c * 128, 128)], locsem.at[w]).start()
    META[ex, 0:8, :] = idt[...].astype(F32)
    META[ex, 8:16, :] = gpt[...]
    META[ex, 16:17, :] = seq[...].astype(F32)
    META[ex, 17:18, :] = ratio[...]

    def fetch_weights():
        for k, (src, r0, r1) in enumerate(((wg, 0, 384), (wu, 192, 576), (wd, 768, 960))):
            for y in range(4):
                mine = pl.multiple_of(y * 1024 + core * 512, 512)
                theirs = pl.multiple_of(y * 1024 + (1 - core) * 512, 512)
                pltpu.make_async_copy(
                    src.at[:, :, pl.ds(mine, 512)], W.at[:, pl.ds(r0, 192), pl.ds(y * 512, 512)], wl.at[0]).start()
                pltpu.make_async_remote_copy(
                    src.at[:, :, pl.ds(theirs, 512)], W.at[:, pl.ds(r1, 192), pl.ds(y * 512, 512)],
                    ws.at[0], wr.at[0], partner, device_id_type=MESH).start()

    def settle_weights():
        for sem in (wl, ws, wr):
            settle(W.at[:, pl.ds(0, 576)], sem.at[0])

    pl.semaphore_wait(bar, 22)
    for w in range(2):
        settle(G.at[w, me], locsem.at[w])

    def origin(s, p, j):
        q = list(pos)
        o = ORDER[p]
        if s >= 1:
            q = shift(q, o[0], j % 4)
        if s == 2:
            q = shift(q, o[1], j // 4)
        return q

    def slot(s, k):
        return (0, 1, 5)[s] + k

    def full_sem(v, p, way, k):
        return ((v * 3 + p) * 2 + way) * 10 + k

    def half_sem(v, p, way, k):
        return ((v * 3 + p) * 2 + way) * 6 + k

    def sent_sem(v, p, way):
        return (v * 3 + p) * 2 + way

    def half_rows(p, way, v=0):
        r0, n, h = PARTS[v][p]
        return pl.ds(r0, h) if way == 0 else pl.ds(r0 + h, n - h)

    def half_count(v, p, way):
        return PARTS[v][p][2] if way == 0 else PARTS[v][p][1] - PARTS[v][p][2]

    def part_rows(p, v=0):
        return pl.ds(PARTS[v][p][0], PARTS[v][p][1])

    def full(v, s, p, j, way):
        ref = G.at[v, blk(origin(s, p, j)), part_rows(p, v)]
        k = slot(s, j // 4 if s == 2 else j)
        return pltpu.make_async_remote_copy(
            ref, ref, sent.at[sent_sem(v, p, way)], fr.at[full_sem(v, p, way, k)], nbr[ORDER[p][s]][way],
            device_id_type=MESH)

    def half(v, s, p, j, way):
        a = ORDER[p][s]
        b = blk(shift(origin(s, p, j), a, 3 if way == 0 else 1))
        ref = G.at[v, b, half_rows(p, way, v)]
        k = 5 if s == 2 else slot(s, j)
        return pltpu.make_async_remote_copy(
            ref, ref, sent.at[sent_sem(v, p, way)], hr.at[half_sem(v, p, way, k)], nbr[a][way],
            device_id_type=MESH)

    def each(f):
        for p in range(3):
            for way in range(2):
                f(p, way)

    def odd(f):
        def body(i, c):
            f(1 + 2 * i)
            return c
        lax.fori_loop(0, 2, body, 0)

    def loop(lo, hi, f):
        def body(i, c):
            f(i)
            return c
        lax.fori_loop(lo, hi, body, 0)

    def send(v, s, j):
        each(lambda p, w: full(v, s, p, j, w).start())

    def hop(v, s, j):
        def one(p, w):
            full(v, s, p, j, w).wait_recv()
            half(v, s, p, j, w).start()
        each(one)

    def hop_bundle(v, b):
        for p in range(3):
            for w in range(2):
                settle(G.at[v, pl.ds(0, 4), part_rows(p, v)], fr.at[full_sem(v, p, w, slot(2, b))])
                loop(0, 4, lambda a, p=p, w=w: half(v, 2, p, group(a, b), w).start())

    def last(v, s, j):
        each(lambda p, w: half(v, s, p, j, w).wait_recv())

    def gather_events(v):
        ev = []
        ev.append(lambda: (send(v, 0, 0), send(v, 1, 0), send(v, 2, 0)))
        ev.append(lambda: (hop(v, 0, 0), odd(lambda a: send(v, 1, a)), odd(lambda a: send(v, 2, group(a, 0)))))
        ev.append(lambda: (hop(v, 1, 0), odd(lambda b: send(v, 2, group(0, b)))))
        ev.append(lambda: (last(v, 0, 0), send(v, 1, 2), send(v, 2, group(2, 0))))
        ev.append(lambda: odd(lambda a: (hop(v, 1, a), odd(lambda b: send(v, 2, group(a, b))))))
        ev.append(lambda: (last(v, 1, 0), send(v, 2, group(0, 2))))
        ev.append(lambda: hop_bundle(v, 0))
        ev.append(lambda: (hop(v, 1, 2), odd(lambda b: send(v, 2, group(2, b)))))
        ev.append(lambda: odd(lambda a: (last(v, 1, a), send(v, 2, group(a, 2)))))
        ev.append(lambda: (last(v, 1, 2), send(v, 2, group(2, 2))))
        ev.append(lambda: odd(lambda b: hop_bundle(v, b)))
        ev.append(lambda: hop_bundle(v, 2))
        return ev

    def early_events(v):
        ev = []
        ev.append(lambda: (send(v, 0, 0), send(v, 1, 0)))
        ev.append(lambda: (hop(v, 0, 0), odd(lambda a: send(v, 1, a))))
        ev.append(lambda: hop(v, 1, 0))
        ev.append(lambda: (last(v, 0, 0), send(v, 1, 2)))
        ev.append(lambda: odd(lambda a: hop(v, 1, a)))
        ev.append(lambda: (last(v, 1, 0), hop(v, 1, 2)))
        ev.append(lambda: (odd(lambda a: last(v, 1, a)), last(v, 1, 2)))
        return ev

    def late_sends(v, b):
        loop(0, 4, lambda a: send(v, 2, group(a, b)))

    def gather_rest(v):
        def one(p, w):
            settle(G.at[v, pl.ds(0, 16), pl.ds(0, half_count(v, p, w))], hr.at[half_sem(v, p, w, 5)])
        each(one)

    def all_sent(v):
        def one(p, w):
            settle(G.at[v, pl.ds(0, 21), pl.ds(0, PARTS[v][p][1] + half_count(v, p, w))], sent.at[sent_sem(v, p, w)])
        each(one)

    def meta_copy(i):
        return pltpu.make_async_remote_copy(
            META.at[ex], META.at[ex], ms.at[0], mr.at[0], (dp, (ex + i) % 16), device_id_type=MESH)

    first = (ex * 4).astype(F32)

    def pair_ids(q):
        return jnp.concatenate([META[2 * q, 0:8], META[2 * q + 1, 0:8]], axis=1)

    def prepare():
        sid = META[:, 16, :]
        lr = META[:, 17, :]
        tw = jnp.zeros((16, 128), F32)
        for s in range(SEQS):
            hit = (sid == float(s)).astype(F32)
            total = jnp.sum(jnp.sum(hit * lr, axis=1, keepdims=True), axis=0, keepdims=True)
            count = jnp.sum(jnp.sum(hit, axis=1, keepdims=True), axis=0, keepdims=True)
            wt = adv[s] * jnp.clip(jnp.exp(total / count), clip_low, clip_high)
            tw = tw + hit * wt
        r = lax.broadcasted_iota(jnp.int32, (256, 256), 0)
        t = lax.broadcasted_iota(jnp.int32, (256, 256), 1)
        earlier = ((r < t) & ((r >= 128) == (t >= 128))).astype(F32).astype(BF)
        row = lax.broadcasted_iota(jnp.int32, (2 * CAP, 256), 0)
        lane = lax.broadcasted_iota(jnp.int32, (2 * CAP, 256), 1)
        second = row >= CAP
        same = second == (lane >= 128)
        slot = (row - jnp.where(second, CAP, 0)).astype(F32)
        for q in range(8):
            ids = pair_ids(q)
            gp = jnp.concatenate([META[2 * q, 8:16], META[2 * q + 1, 8:16]], axis=1)
            twq = jnp.concatenate([tw[2 * q:2 * q + 1], tw[2 * q + 1:2 * q + 2]], axis=1)
            hot, cw = [], []
            for n in range(4):
                hit = (ids == first + float(n)).astype(F32)
                hot.append(jnp.sum(hit, axis=0, keepdims=True))
                cw.append(jnp.sum(hit * gp, axis=0, keepdims=True) * twq)
            hots = jnp.concatenate(hot + hot, axis=0)
            rank = jnp.dot(hots.astype(BF), earlier, preferred_element_type=F32)
            for n in range(4):
                sel = same & (rank[n:n + 1] == slot) & (hot[n] > 0.5)
                pick = sel.astype(F32)
                PM[q, n * 48:(n + 1) * 48, :] = pick.astype(BF)
                cc = jnp.sum(pick * cw[n], axis=1, keepdims=True)
                CC[q, n * 48:(n + 1) * 48, :] = jnp.broadcast_to(cc, (48, 128))
            PT[q] = PM[q].T

    def select(v, q):
        dst = XS if v == 0 else DY
        rows = pl.ds(pl.multiple_of(q * 48, 16), 48)
        pm = PM[q]
        for y in range(4):
            xp = jnp.concatenate([
                jnp.concatenate([G[v, (2 * q + b) * 4 + y, c * 128:(c + 1) * 128, :] for c in range(4)], axis=1)
                for b in range(2)], axis=0)
            r = jnp.dot(pm, xp, preferred_element_type=F32)
            if v == 1:
                r = r * CC[q, :, 0:1]
            r = r.astype(BF)
            for n in range(4):
                dst[n, rows, y * 512:(y + 1) * 512] = r[n * 48:(n + 1) * 48]

    def swap_gu(n):
        return pltpu.make_async_remote_copy(
            SND.at[n, pl.ds(0, 384)], RCV.at[n, pl.ds(0, 384)], es.at[0], er.at[n], partner, device_id_type=MESH)

    def swap_z(n):
        return pltpu.make_async_remote_copy(
            SND.at[n, pl.ds(384, 192)], RCV.at[n, pl.ds(384, 192)], es.at[0], er.at[4 + n], partner,
            device_id_type=MESH)

    def gate_up(n):
        x = XS[n]
        OWN[n, 0:384] = lax.dot_general(W[n, 0:384], x, NT, preferred_element_type=F32)
        SND[n, 0:384] = lax.dot_general(W[n, 384:768], x, NT, preferred_element_type=F32).astype(BF)
        swap_gu(n).start()

    def down(n):
        z = lax.dot_general(W[n, 768:1152], DY[n], NT, preferred_element_type=F32)
        OWN[n, 384:576] = z[0:192]
        SND[n, 384:576] = z[192:384].astype(BF)
        swap_z(n).start()

    def swap_d(n):
        return pltpu.make_async_remote_copy(
            DT.at[n, :, pl.ds(0, 384)], DT.at[n, :, pl.ds(384, 384)], ts.at[0], tr.at[n], partner,
            device_id_type=MESH)

    def swap_h(n):
        return pltpu.make_async_remote_copy(
            HID.at[n, pl.ds(0, 192)], HID.at[n, pl.ds(192, 192)], ts.at[1], th.at[0], partner,
            device_id_type=MESH)

    def hidden(n):
        swap_gu(n).wait_recv()
        g = OWN[n, 0:192] + RCV[n, 0:192].astype(F32)
        u = OWN[n, 192:384] + RCV[n, 192:384].astype(F32)
        sg = jax.nn.sigmoid(g)
        gsg = g * sg
        HID[n, 0:192] = (gsg * u).astype(BF)
        OWN[n, 0:192] = u * sg * (1.0 + g * (1.0 - sg))
        OWN[n, 192:384] = gsg
        swap_h(n).start()

    def middle(n):
        swap_z(n).wait_recv()
        z = OWN[n, 384:576] + RCV[n, 384:576].astype(F32)
        d = jnp.concatenate([OWN[n, 0:192] * z, OWN[n, 192:384] * z], axis=0).astype(BF)
        DT[n, :, 0:384] = d.T
        swap_d(n).start()
        GROW[n] = jnp.broadcast_to(jnp.sum(HID[n, 0:192].astype(F32) * z, axis=0, keepdims=True), (8, 384))

    def grad_x(n, y):
        cols = pl.ds(pl.multiple_of(y * 512, 512), 512)
        XS[n, :, cols] = jnp.dot(DT[n], W[n, 0:768, cols], preferred_element_type=F32).astype(BF)

    def scatter(q, y):
        rows = pl.ds(pl.multiple_of(q * 48, 16), 48)
        cols = pl.ds(pl.multiple_of(y * 512, 512), 512)
        part = jnp.concatenate([XS[n, rows, cols] for n in range(4)], axis=0)
        r = jnp.dot(PT[q], part, preferred_element_type=F32).astype(BF)
        for b in range(2):
            for c in range(4):
                G[0, (2 * q + b) * 4 + y, c * 128:(c + 1) * 128, :] = (
                    r[b * 128:(b + 1) * 128, c * 128:(c + 1) * 128])

    def out_local(n, y):
        cols = pl.multiple_of(y * 1024 + core * 512, 512)
        return pltpu.make_async_copy(
            XS.at[n, pl.ds(0, 192), pl.ds(y * 512, 512)], gd.at[n, :, pl.ds(cols, 512)], ol.at[0])

    def out_remote(n, y):
        cols = pl.multiple_of(y * 1024 + core * 512, 512)
        return pltpu.make_async_remote_copy(
            XS.at[n, pl.ds(192, 192), pl.ds(y * 512, 512)], gd.at[n, :, pl.ds(cols, 512)],
            osnd.at[0], orcv.at[0], partner, device_id_type=MESH)

    def grad_down(n):
        h = HID[n]
        for y in range(4):
            cols = slice(y * 512, (y + 1) * 512)
            XS[n, :, cols] = jnp.dot(h, DY[n, :, cols], preferred_element_type=F32).astype(BF)
            out_local(n, y).start()
            out_remote(n, y).start()

    def gate_tokens():
        lane = lax.broadcasted_iota(jnp.int32, (8, 192), 1)
        row = lax.broadcasted_iota(jnp.int32, (8, 192), 0)
        own = (lane >= row * 48) & (lane < row * 48 + 48)
        for q in range(8):
            vals = jnp.concatenate([GROW[n, 0:1, q * 48:(q + 1) * 48] for n in range(4)], axis=1)
            a = jnp.where(own, vals, 0.0)
            gt = jnp.dot(a, PM[q].astype(F32), precision=lax.Precision.HIGHEST, preferred_element_type=F32)
            ids = pair_ids(q)
            r = jnp.zeros((8, 256), F32)
            for n in range(4):
                r = r + jnp.where(ids == first + float(n), gt[n:n + 1], 0.0)
            GS[2 * q] = r[:, 0:128]
            GS[2 * q + 1] = r[:, 128:256]

    def gate_one(i):
        e = (ex + i) % 16
        return pltpu.make_async_remote_copy(
            GS.at[e], GR.at[i], gs1.at[0], gr1.at[0], (dp, e), device_id_type=MESH)

    def gate_two(i):
        return pltpu.make_async_remote_copy(
            GT, GX.at[i], gs2.at[0], gr2.at[0], ((dp + i) % 8, ex), device_id_type=MESH)

    def member(p, k, i):
        return group(k, i) if p == 1 else group(i, k)

    def rhalf(s, p, j, way, k=0):
        a = ORDER[p][s]
        b = blk(shift(origin(s, p, j), a, 2))
        rows = half_rows(p, way)
        sem = slot(2, k) if s == 2 else slot(s, j)
        return pltpu.make_async_remote_copy(
            G.at[0, b, rows], G.at[1, BASE[s] + j, rows], sent.at[sent_sem(0, p, way)],
            fr.at[full_sem(0, p, way, sem)], nbr[a][way], device_id_type=MESH)

    def rfull(s, p, j, way, k=0):
        a = ORDER[p][s]
        b = blk(shift(origin(s, p, j), a, 1 if way == 0 else 3))
        rows = part_rows(p)
        sem = slot(2, k) if s == 2 else slot(s, j)
        return pltpu.make_async_remote_copy(
            G.at[0, b, rows], G.at[1, 21 + (BASE[s] + j) * 2 + way, rows], sent.at[sent_sem(0, p, way)],
            fr.at[full_sem(1, p, way, sem)], nbr[a][way], device_id_type=MESH)

    def add_half(s, p, j, way, f=0):
        k = blk(shift(origin(s, p, j), ORDER[p][s], 1 if way == 0 else 3))
        rows = half_rows(p, way)
        G[0, k, rows] = (G[0, k, rows].astype(F32) + G[1, BASE[s] + j, rows].astype(F32)).astype(BF)
        rfull(s, p, j, way, f).start()

    def add_full(s, p, j):
        k = blk(origin(s, p, j))
        rows = part_rows(p)
        f = 21 + (BASE[s] + j) * 2
        G[0, k, rows] = (G[0, k, rows].astype(F32) + (
            G[1, f, rows].astype(F32) + G[1, f + 1, rows].astype(F32))).astype(BF)

    def start2(p, k):
        def one(i):
            rhalf(2, p, member(p, k, i), 0, k).start()
            rhalf(2, p, member(p, k, i), 1, k).start()
        loop(0, 4, one)

    def halves_in(p, k):
        for w in range(2):
            settle(G.at[1, pl.ds(0, 4), half_rows(p, w)], fr.at[full_sem(0, p, w, slot(2, k))])

    def pass_on(p, k, i, f):
        for w in range(2):
            add_half(2, p, member(p, k, i), w, f)

    def mid2(p, step):
        if step == 0:
            halves_in(p, 2)
            loop(0, 4, lambda i: pass_on(p, 2, (i + 2) % 4, 0))
        elif step == 1:
            halves_in(p, 3)
            loop(1, 4, lambda i: pass_on(p, 3, i, 1))
        elif step == 2:
            halves_in(p, 1)
            loop(1, 4, lambda i: pass_on(p, 1, i, 1))
        elif step == 3:
            halves_in(p, 0)
            pass_on(p, 0, 2, 2)
        elif step == 4:
            odd(lambda k: pass_on(p, k, 0, 3))
            odd(lambda i: pass_on(p, 0, i, 3))
        else:
            pass_on(p, 0, 0, 4)

    def end2(p, f):
        n = (4, 6, 1, 4, 1)[f]
        for w in range(2):
            settle(G.at[1, pl.ds(0, n), part_rows(p)], fr.at[full_sem(1, p, w, slot(2, f))])
        take = lambda k, i: add_full(2, p, member(p, k, i))
        if f == 0:
            loop(0, 4, lambda i: take(2, i))
        elif f == 1:
            odd(lambda k: loop(1, 4, lambda i: take(k, i)))
        elif f == 2:
            take(0, 2)
        elif f == 3:
            odd(lambda k: take(k, 0))
            odd(lambda i: take(0, i))
        else:
            take(0, 0)

    def start(s, p, j):
        for w in range(2):
            rhalf(s, p, j, w).start()

    def mid(s, p, j):
        for w in range(2):
            rhalf(s, p, j, w).wait_recv()
            add_half(s, p, j, w)

    def end(s, p, j):
        for w in range(2):
            rfull(s, p, j, w).wait_recv()
        add_full(s, p, j)

    far = (2, 3, 1, 0)
    for i in range(1, 16):
        meta_copy(i).start()
    ev0 = gather_events(0)
    ev1 = early_events(1)
    ev0[0]()
    fetch_weights()
    ev0[1]()
    ev0[2]()
    ev0[3]()
    settle(META.at[pl.ds(0, 15)], mr.at[0])
    settle(META.at[pl.ds(0, 15)], ms.at[0])
    ev1[0]()
    ev0[4]()
    ev0[5]()
    ev1[1]()
    ev0[6]()
    prepare()
    ev1[2]()
    ev0[7]()
    ev1[3]()
    ev0[8]()
    ev1[4]()
    ev0[9]()
    ev1[5]()
    ev0[10]()
    ev1[6]()
    ev0[11]()
    for b in (0, 1, 3, 2):
        late_sends(1, b)
    gather_rest(0)
    loop(0, 4, lambda q: select(0, q))
    hop_bundle(1, 0)
    loop(4, 8, lambda q: select(0, q))
    settle_weights()
    hop_bundle(1, 1)
    loop(0, 2, gate_up)
    hop_bundle(1, 3)
    loop(2, 4, gate_up)
    loop(0, 2, hidden)
    hop_bundle(1, 2)
    loop(2, 4, hidden)
    gather_rest(1)
    loop(0, 8, lambda q: select(1, q))
    all_sent(0)
    all_sent(1)
    for a in range(3):
        for n in nbr[a]:
            pl.semaphore_signal(ready, inc=1, device_id=n, device_id_type=MESH)
    loop(0, 4, down)
    loop(0, 4, middle)
    loop(0, 4, lambda n: swap_d(n).wait_recv())

    def columns(b):
        y = (pos[1] + b) % 4
        loop(0, 4, lambda n: grad_x(n, y))
        loop(0, 8, lambda q: scatter(q, y))

    columns(2)
    pl.semaphore_wait(ready, 6)
    start2(0, 2)
    start2(1, 2)
    start2(2, 2)
    columns(3)
    start2(0, 3)
    start2(1, 3)
    start2(2, 3)
    columns(1)
    start2(0, 1)
    start2(1, 1)
    start2(2, 1)
    for p in range(3):
        mid2(p, 0)
    columns(0)
    start2(0, 0)
    start2(1, 0)
    start2(2, 0)
    for p in range(3):
        end2(p, 0)
        if p == 1:
            start(1, 1, 2)
        else:
            loop(0, 4, lambda a, p=p: start(1, p, (a + 2) % 4))
    for p in range(3):
        mid2(p, 1)
    gate_tokens()
    for i in range(1, 16):
        gate_one(i).start()
    for p in range(3):
        mid2(p, 2)
    mid(1, 1, 2)
    for p in range(3):
        mid2(p, 3)
    settle(HID.at[:, pl.ds(0, 192)], th.at[0])
    loop(0, 4, grad_down)
    for p in range(3):
        end2(p, 1)
        if p == 1:
            odd(lambda a: start(1, 1, a))
        else:
            loop(1, 4, lambda a, p=p: mid(1, p, a))
    for p in range(3):
        mid2(p, 4)
    settle(GR.at[pl.ds(0, 15)], gr1.at[0])
    acc = GS[ex]
    for i in range(1, 16):
        acc = acc + GR[i]
    GT[...] = acc
    for i in range(1, 8):
        gate_two(i).start()
    for p in range(3):
        end2(p, 2)
        if p == 1:
            start(1, 1, 0)
        end(1, p, 2)
        start(0, p, 0)
    for p in range(3):
        mid2(p, 5)
    odd(lambda a: mid(1, 1, a))
    for p in range(3):
        end2(p, 3)
        mid(1, p, 0)
        odd(lambda a, p=p: end(1, p, a))
        mid(0, p, 0)
    for p in range(3):
        end2(p, 4)
        end(1, p, 0)
    settle(GX.at[pl.ds(0, 7)], gr2.at[0])
    acc = GT[...]
    for i in range(1, 8):
        acc = acc + GX[i]
    gates[...] = acc / gpt[...]
    for p in range(3):
        end(0, p, 0)
    for c in range(4):
        dxo[:, c * 128:(c + 1) * 128] = G[0, me, c * 128:(c + 1) * 128, :]
    all_sent(0)
    settle(GR.at[pl.ds(0, 15)], gs1.at[0])
    settle(GX.at[pl.ds(0, 7)], gs2.at[0])
    settle(SND, es.at[0])
    settle(DT.at[:, :, pl.ds(0, 384)], ts.at[0])
    settle(HID.at[:, pl.ds(0, 192)], ts.at[1])
    for sem in (ol, osnd, orcv):
        settle(XS.at[:, pl.ds(0, 192)], sem.at[0])


def store_kernel(gd, dx, gt, gdo, dxo, gto, B, DB, GB, arrive, leave):
    pairs = [(gd.at[i // 4, pl.ds(i % 4 * 48, 48)], B.at[i], gdo.at[i // 4, pl.ds(i % 4 * 48, 48)]) for i in range(16)]
    pairs += [(dx, DB, dxo), (gt, GB, gto)]
    for i, (src, buf, dst) in enumerate(pairs):
        pltpu.make_async_copy(src, buf, arrive.at[i]).start()
    for i, (src, buf, dst) in enumerate(pairs):
        pltpu.make_async_copy(src, buf, arrive.at[i]).wait()
        pltpu.make_async_copy(buf, dst, leave.at[i]).start()
    for i, (src, buf, dst) in enumerate(pairs):
        pltpu.make_async_copy(buf, dst, leave.at[i]).wait()


def on_device(
    tokens, grad_out, expert_ids, gate_probs, seq_ids, log_ratio, advantages, w_gate, w_up, w_down
):
    vmem = pl.BlockSpec(memory_space=pltpu.VMEM)
    hbm = pl.BlockSpec(memory_space=pl.ANY)
    dma = lambda n: pltpu.SemaphoreType.DMA((n,))
    dx, gates, gd = pl.pallas_call(
        step_kernel,
        out_shape=(
            jax.ShapeDtypeStruct((128, 512), BF),
            jax.ShapeDtypeStruct((8, 128), F32),
            jax.ShapeDtypeStruct((4, 192, 4096), BF),
        ),
        in_specs=[pl.BlockSpec(memory_space=pltpu.SMEM)] + [vmem] * 6 + [hbm] * 3,
        out_specs=(vmem, vmem, hbm),
        scratch_shapes=[
            pltpu.VMEM((2, 64, 512, 128), BF),
            pltpu.VMEM((4, 384, 2048), BF),
            pltpu.VMEM((4, 384, 2048), BF),
            pltpu.VMEM((4, 1152, 2048), BF),
            pltpu.VMEM((4, 576, 384), F32),
            pltpu.VMEM((4, 576, 384), BF),
            pltpu.VMEM((4, 576, 384), BF),
            pltpu.VMEM((4, 384, 768), BF),
            pltpu.VMEM((4, 384, 384), BF),
            pltpu.VMEM((8, 192, 256), BF),
            pltpu.VMEM((8, 256, 192), BF),
            pltpu.VMEM((8, 192, 128), F32),
            pltpu.VMEM((16, 24, 128), F32),
            pltpu.VMEM((4, 8, 384), F32),
            pltpu.VMEM((16, 8, 128), F32),
            pltpu.VMEM((16, 8, 128), F32),
            pltpu.VMEM((8, 128), F32),
            pltpu.VMEM((8, 8, 128), F32),
            dma(2), dma(12), dma(120), dma(72), dma(1), dma(1), dma(1), dma(1), dma(1),
            dma(1), dma(8), dma(2), dma(4), dma(1), dma(1), dma(1), dma(1), dma(1), dma(1), dma(1), dma(1),
            pltpu.SemaphoreType.REGULAR,
        ],
        compiler_params=pltpu.CompilerParams(
            collective_id=0, has_side_effects=True, vmem_limit_bytes=67043328),
        name="expert_step",
    )(
        advantages, tokens, grad_out, expert_ids.T, gate_probs.T, seq_ids.reshape(1, -1), log_ratio.reshape(1, -1),
        w_gate, w_up, w_down)
    gd, dx, gates = pl.pallas_call(
        store_kernel,
        out_shape=(
            jax.ShapeDtypeStruct((4, 192, 4096), BF),
            jax.ShapeDtypeStruct((128, 512), BF),
            jax.ShapeDtypeStruct((8, 128), F32),
        ),
        in_specs=[hbm] * 3,
        out_specs=(hbm,) * 3,
        scratch_shapes=[
            pltpu.VMEM((16, 48, 4096), BF), pltpu.VMEM((128, 512), BF), pltpu.VMEM((8, 128), F32), dma(18), dma(18),
        ],
        name="store_results",
    )(gd, dx, gates)
    return dx, gates.T, gd


def solution(mesh):
    return jax.shard_map(
        on_device,
        mesh=mesh,
        in_specs=(
            P("expert", "dp"),
            P("expert", "dp"),
            P("expert", None),
            P("expert", None),
            P("expert"),
            P("expert"),
            P(),
            P("expert", "dp", None),
            P("expert", "dp", None),
            P("expert", "dp", None),
        ),
        out_specs=(P("expert", "dp"), P("expert", None), P("expert", "dp", None)),
        check_vma=False,
    )
```

```python
import jax
import jax.numpy as jnp
from jax import lax
from jax.experimental import pallas as pl
from jax.experimental.pallas import tpu as pltpu
from jax.sharding import PartitionSpec as P

SEQS = 8
TOP = 8
CAP = 24
clip_low = 0.9
clip_high = 1.1

MESH = pl.DeviceIdType.MESH
BF = jnp.bfloat16
F32 = jnp.float32
PARTS = (
    ((0, 176, 96), (176, 176, 80), (352, 160, 80)),
    ((0, 176, 80), (176, 160, 80), (336, 176, 96)),
)
ORDER = ((0, 1, 2), (1, 2, 0), (2, 0, 1))
BASE = (0, 1, 5)
COUNT = (1, 4, 16)
NT = (((1,), (1,)), ((), ()))
TN = (((0,), (0,)), ((), ()))


def group(a, b):
    return b * 4 + a


def step_kernel(
    adv, tok, gout, idt, gpt, seq, ratio, wg, wu, wd,
    dxo, gates, gd,
    G, XS, DY, W, OWN, SND, RCV, DT, HID, PM, PT, CC, META, GROW, GS, GR, GT, GX,
    locsem, sent, fr, hr, wl, ws, wr, ms, mr,
    es, er, ts, tr, th, gs1, gr1, gs2, gr2, ol, osnd, orcv, ready,
):
    dp = lax.axis_index("dp")
    ex = lax.axis_index("expert")
    pos = [ex % 4, dp // 2, ex // 4]
    core = dp % 2

    def dev(q, c):
        return (q[1] * 2 + c, q[2] * 4 + q[0])

    def shift(q, a, n):
        q = list(q)
        q[a] = (q[a] + n) % 4
        return q

    def blk(q):
        return (q[2] * 4 + q[0]) * 4 + q[1]

    nbr = [(dev(shift(pos, a, 1), core), dev(shift(pos, a, 3), core)) for a in range(3)]
    partner = (pos[1] * 2 + 1 - core, ex)
    me = blk(pos)
    bar = pltpu.get_barrier_semaphore()
    for i in range(1, 16):
        pl.semaphore_signal(bar, inc=1, device_id=(dp, (ex + i) % 16), device_id_type=MESH)
    for i in range(1, 8):
        pl.semaphore_signal(bar, inc=1, device_id=((dp + i) % 8, ex), device_id_type=MESH)

    def settle(ref, sem):
        pltpu.make_async_copy(ref, ref, sem).wait()

    for c in range(4):
        for w, src in enumerate((tok, gout)):
            pltpu.make_async_copy(
                src.at[:, pl.ds(c * 128, 128)], G.at[w, me, pl.ds(c * 128, 128)], locsem.at[w]).start()
    META[ex, 0:8, :] = idt[...].astype(F32)
    META[ex, 8:16, :] = gpt[...]
    META[ex, 16:17, :] = seq[...].astype(F32)
    META[ex, 17:18, :] = ratio[...]

    def fetch_weights():
        for k, (src, r0, r1) in enumerate(((wg, 0, 384), (wu, 192, 576), (wd, 768, 960))):
            for y in range(4):
                mine = pl.multiple_of(y * 1024 + core * 512, 512)
                theirs = pl.multiple_of(y * 1024 + (1 - core) * 512, 512)
                pltpu.make_async_copy(
                    src.at[:, :, pl.ds(mine, 512)], W.at[:, pl.ds(r0, 192), pl.ds(y * 512, 512)], wl.at[0]).start()
                pltpu.make_async_remote_copy(
                    src.at[:, :, pl.ds(theirs, 512)], W.at[:, pl.ds(r1, 192), pl.ds(y * 512, 512)],
                    ws.at[0], wr.at[0], partner, device_id_type=MESH).start()

    def settle_weights():
        for sem in (wl, ws, wr):
            settle(W.at[:, pl.ds(0, 576)], sem.at[0])

    pl.semaphore_wait(bar, 22)
    for w in range(2):
        settle(G.at[w, me], locsem.at[w])

    def origin(s, p, j):
        q = list(pos)
        o = ORDER[p]
        if s >= 1:
            q = shift(q, o[0], j % 4)
        if s == 2:
            q = shift(q, o[1], j // 4)
        return q

    def slot(s, k):
        return (0, 1, 5)[s] + k

    def full_sem(v, p, way, k):
        return ((v * 3 + p) * 2 + way) * 10 + k

    def half_sem(v, p, way, k):
        return ((v * 3 + p) * 2 + way) * 6 + k

    def sent_sem(v, p, way):
        return (v * 3 + p) * 2 + way

    def half_rows(p, way, v=0):
        r0, n, h = PARTS[v][p]
        return pl.ds(r0, h) if way == 0 else pl.ds(r0 + h, n - h)

    def half_count(v, p, way):
        return PARTS[v][p][2] if way == 0 else PARTS[v][p][1] - PARTS[v][p][2]

    def part_rows(p, v=0):
        return pl.ds(PARTS[v][p][0], PARTS[v][p][1])

    def full(v, s, p, j, way):
        ref = G.at[v, blk(origin(s, p, j)), part_rows(p, v)]
        k = slot(s, j // 4 if s == 2 else j)
        return pltpu.make_async_remote_copy(
            ref, ref, sent.at[sent_sem(v, p, way)], fr.at[full_sem(v, p, way, k)], nbr[ORDER[p][s]][way],
            device_id_type=MESH)

    def half(v, s, p, j, way):
        a = ORDER[p][s]
        b = blk(shift(origin(s, p, j), a, 3 if way == 0 else 1))
        ref = G.at[v, b, half_rows(p, way, v)]
        k = 5 if s == 2 else slot(s, j)
        return pltpu.make_async_remote_copy(
            ref, ref, sent.at[sent_sem(v, p, way)], hr.at[half_sem(v, p, way, k)], nbr[a][way],
            device_id_type=MESH)

    def each(f):
        for p in range(3):
            for way in range(2):
                f(p, way)

    def odd(f):
        def body(i, c):
            f(1 + 2 * i)
            return c
        lax.fori_loop(0, 2, body, 0)

    def loop(lo, hi, f):
        def body(i, c):
            f(i)
            return c
        lax.fori_loop(lo, hi, body, 0)

    def send(v, s, j):
        each(lambda p, w: full(v, s, p, j, w).start())

    def hop(v, s, j):
        def one(p, w):
            full(v, s, p, j, w).wait_recv()
            half(v, s, p, j, w).start()
        each(one)

    def hop_bundle(v, b):
        for p in range(3):
            for w in range(2):
                settle(G.at[v, pl.ds(0, 4), part_rows(p, v)], fr.at[full_sem(v, p, w, slot(2, b))])
                loop(0, 4, lambda a, p=p, w=w: half(v, 2, p, group(a, b), w).start())

    def last(v, s, j):
        each(lambda p, w: half(v, s, p, j, w).wait_recv())

    def gather_events(v):
        ev = []
        ev.append(lambda: (send(v, 0, 0), send(v, 1, 0), send(v, 2, 0)))
        ev.append(lambda: (hop(v, 0, 0), odd(lambda a: send(v, 1, a)), odd(lambda a: send(v, 2, group(a, 0)))))
        ev.append(lambda: (hop(v, 1, 0), odd(lambda b: send(v, 2, group(0, b)))))
        ev.append(lambda: (last(v, 0, 0), send(v, 1, 2), send(v, 2, group(2, 0))))
        ev.append(lambda: odd(lambda a: (hop(v, 1, a), odd(lambda b: send(v, 2, group(a, b))))))
        ev.append(lambda: (last(v, 1, 0), send(v, 2, group(0, 2))))
        ev.append(lambda: hop_bundle(v, 0))
        ev.append(lambda: (hop(v, 1, 2), odd(lambda b: send(v, 2, group(2, b)))))
        ev.append(lambda: odd(lambda a: (last(v, 1, a), send(v, 2, group(a, 2)))))
        ev.append(lambda: (last(v, 1, 2), send(v, 2, group(2, 2))))
        ev.append(lambda: odd(lambda b: hop_bundle(v, b)))
        ev.append(lambda: hop_bundle(v, 2))
        return ev

    def early_events(v):
        ev = []
        ev.append(lambda: (send(v, 0, 0), send(v, 1, 0)))
        ev.append(lambda: (hop(v, 0, 0), odd(lambda a: send(v, 1, a))))
        ev.append(lambda: hop(v, 1, 0))
        ev.append(lambda: (last(v, 0, 0), send(v, 1, 2)))
        ev.append(lambda: odd(lambda a: hop(v, 1, a)))
        ev.append(lambda: (last(v, 1, 0), hop(v, 1, 2)))
        ev.append(lambda: (odd(lambda a: last(v, 1, a)), last(v, 1, 2)))
        return ev

    def late_sends(v, b):
        loop(0, 4, lambda a: send(v, 2, group(a, b)))

    def gather_rest(v):
        def one(p, w):
            settle(G.at[v, pl.ds(0, 16), pl.ds(0, half_count(v, p, w))], hr.at[half_sem(v, p, w, 5)])
        each(one)

    def all_sent(v):
        def one(p, w):
            settle(G.at[v, pl.ds(0, 21), pl.ds(0, PARTS[v][p][1] + half_count(v, p, w))], sent.at[sent_sem(v, p, w)])
        each(one)

    def meta_copy(i):
        return pltpu.make_async_remote_copy(
            META.at[ex], META.at[ex], ms.at[0], mr.at[0], (dp, (ex + i) % 16), device_id_type=MESH)

    first = (ex * 4).astype(F32)

    def pair_ids(q):
        return jnp.concatenate([META[2 * q, 0:8], META[2 * q + 1, 0:8]], axis=1)

    def prepare():
        sid = META[:, 16, :]
        lr = META[:, 17, :]
        tw = jnp.zeros((16, 128), F32)
        for s in range(SEQS):
            hit = (sid == float(s)).astype(F32)
            total = jnp.sum(jnp.sum(hit * lr, axis=1, keepdims=True), axis=0, keepdims=True)
            count = jnp.sum(jnp.sum(hit, axis=1, keepdims=True), axis=0, keepdims=True)
            wt = adv[s] * jnp.clip(jnp.exp(total / count), clip_low, clip_high)
            tw = tw + hit * wt
        r = lax.broadcasted_iota(jnp.int32, (256, 256), 0)
        t = lax.broadcasted_iota(jnp.int32, (256, 256), 1)
        earlier = ((r < t) & ((r >= 128) == (t >= 128))).astype(F32).astype(BF)
        row = lax.broadcasted_iota(jnp.int32, (2 * CAP, 256), 0)
        lane = lax.broadcasted_iota(jnp.int32, (2 * CAP, 256), 1)
        second = row >= CAP
        same = second == (lane >= 128)
        slot = (row - jnp.where(second, CAP, 0)).astype(F32)
        for q in range(8):
            ids = pair_ids(q)
            gp = jnp.concatenate([META[2 * q, 8:16], META[2 * q + 1, 8:16]], axis=1)
            twq = jnp.concatenate([tw[2 * q:2 * q + 1], tw[2 * q + 1:2 * q + 2]], axis=1)
            hot, cw = [], []
            for n in range(4):
                hit = (ids == first + float(n)).astype(F32)
                hot.append(jnp.sum(hit, axis=0, keepdims=True))
                cw.append(jnp.sum(hit * gp, axis=0, keepdims=True) * twq)
            hots = jnp.concatenate(hot + hot, axis=0)
            rank = jnp.dot(hots.astype(BF), earlier, preferred_element_type=F32)
            for n in range(4):
                sel = same & (rank[n:n + 1] == slot) & (hot[n] > 0.5)
                pick = sel.astype(F32)
                PM[q, n * 48:(n + 1) * 48, :] = pick.astype(BF)
                cc = jnp.sum(pick * cw[n], axis=1, keepdims=True)
                CC[q, n * 48:(n + 1) * 48, :] = jnp.broadcast_to(cc, (48, 128))
            PT[q] = PM[q].T

    def select(v, q):
        dst = XS if v == 0 else DY
        rows = pl.ds(pl.multiple_of(q * 48, 16), 48)
        pm = PM[q]
        for y in range(4):
            xp = jnp.concatenate([
                jnp.concatenate([G[v, (2 * q + b) * 4 + y, c * 128:(c + 1) * 128, :] for c in range(4)], axis=1)
                for b in range(2)], axis=0)
            r = jnp.dot(pm, xp, preferred_element_type=F32)
            if v == 1:
                r = r * CC[q, :, 0:1]
            r = r.astype(BF)
            for n in range(4):
                dst[n, rows, y * 512:(y + 1) * 512] = r[n * 48:(n + 1) * 48]

    def swap_gu(n):
        return pltpu.make_async_remote_copy(
            SND.at[n, pl.ds(0, 384)], RCV.at[n, pl.ds(0, 384)], es.at[0], er.at[n], partner, device_id_type=MESH)

    def swap_z(n):
        return pltpu.make_async_remote_copy(
            SND.at[n, pl.ds(384, 192)], RCV.at[n, pl.ds(384, 192)], es.at[0], er.at[4 + n], partner,
            device_id_type=MESH)

    def gate_up(n):
        x = XS[n]
        OWN[n, 0:384] = lax.dot_general(W[n, 0:384], x, NT, preferred_element_type=F32)
        SND[n, 0:384] = lax.dot_general(W[n, 384:768], x, NT, preferred_element_type=F32).astype(BF)
        swap_gu(n).start()

    def down(n):
        z = lax.dot_general(W[n, 768:1152], DY[n], NT, preferred_element_type=F32)
        OWN[n, 384:576] = z[0:192]
        SND[n, 384:576] = z[192:384].astype(BF)
        swap_z(n).start()

    def swap_d(n):
        return pltpu.make_async_remote_copy(
            DT.at[n, :, pl.ds(0, 384)], DT.at[n, :, pl.ds(384, 384)], ts.at[0], tr.at[n], partner,
            device_id_type=MESH)

    def swap_h(n):
        return pltpu.make_async_remote_copy(
            HID.at[n, pl.ds(0, 192)], HID.at[n, pl.ds(192, 192)], ts.at[1], th.at[0], partner,
            device_id_type=MESH)

    def hidden(n):
        swap_gu(n).wait_recv()
        g = OWN[n, 0:192] + RCV[n, 0:192].astype(F32)
        u = OWN[n, 192:384] + RCV[n, 192:384].astype(F32)
        sg = jax.nn.sigmoid(g)
        gsg = g * sg
        HID[n, 0:192] = (gsg * u).astype(BF)
        OWN[n, 0:192] = u * sg * (1.0 + g * (1.0 - sg))
        OWN[n, 192:384] = gsg
        swap_h(n).start()

    def middle(n):
        swap_z(n).wait_recv()
        z = OWN[n, 384:576] + RCV[n, 384:576].astype(F32)
        d = jnp.concatenate([OWN[n, 0:192] * z, OWN[n, 192:384] * z], axis=0).astype(BF)
        DT[n, :, 0:384] = d.T
        swap_d(n).start()
        GROW[n] = jnp.broadcast_to(jnp.sum(HID[n, 0:192].astype(F32) * z, axis=0, keepdims=True), (8, 384))

    def grad_x(n, y):
        cols = pl.ds(pl.multiple_of(y * 512, 512), 512)
        XS[n, :, cols] = jnp.dot(DT[n], W[n, 0:768, cols], preferred_element_type=F32).astype(BF)

    def scatter(q, y):
        rows = pl.ds(pl.multiple_of(q * 48, 16), 48)
        cols = pl.ds(pl.multiple_of(y * 512, 512), 512)
        part = jnp.concatenate([XS[n, rows, cols] for n in range(4)], axis=0)
        r = jnp.dot(PT[q], part, preferred_element_type=F32).astype(BF)
        for b in range(2):
            for c in range(4):
                G[0, (2 * q + b) * 4 + y, c * 128:(c + 1) * 128, :] = (
                    r[b * 128:(b + 1) * 128, c * 128:(c + 1) * 128])

    def out_local(n, y):
        cols = pl.multiple_of(y * 1024 + core * 512, 512)
        return pltpu.make_async_copy(
            XS.at[n, pl.ds(0, 192), pl.ds(y * 512, 512)], gd.at[n, :, pl.ds(cols, 512)], ol.at[0])

    def out_remote(n, y):
        cols = pl.multiple_of(y * 1024 + core * 512, 512)
        return pltpu.make_async_remote_copy(
            XS.at[n, pl.ds(192, 192), pl.ds(y * 512, 512)], gd.at[n, :, pl.ds(cols, 512)],
            osnd.at[0], orcv.at[0], partner, device_id_type=MESH)

    def grad_down(n):
        h = HID[n]
        for y in range(4):
            cols = slice(y * 512, (y + 1) * 512)
            XS[n, :, cols] = jnp.dot(h, DY[n, :, cols], preferred_element_type=F32).astype(BF)
            out_local(n, y).start()
            out_remote(n, y).start()

    def gate_tokens():
        lane = lax.broadcasted_iota(jnp.int32, (8, 192), 1)
        row = lax.broadcasted_iota(jnp.int32, (8, 192), 0)
        own = (lane >= row * 48) & (lane < row * 48 + 48)
        for q in range(8):
            vals = jnp.concatenate([GROW[n, 0:1, q * 48:(q + 1) * 48] for n in range(4)], axis=1)
            a = jnp.where(own, vals, 0.0)
            gt = jnp.dot(a, PM[q].astype(F32), precision=lax.Precision.HIGHEST, preferred_element_type=F32)
            ids = pair_ids(q)
            r = jnp.zeros((8, 256), F32)
            for n in range(4):
                r = r + jnp.where(ids == first + float(n), gt[n:n + 1], 0.0)
            GS[2 * q] = r[:, 0:128]
            GS[2 * q + 1] = r[:, 128:256]

    def gate_one(i):
        e = (ex + i) % 16
        return pltpu.make_async_remote_copy(
            GS.at[e], GR.at[i], gs1.at[0], gr1.at[0], (dp, e), device_id_type=MESH)

    def gate_two(i):
        return pltpu.make_async_remote_copy(
            GT, GX.at[i], gs2.at[0], gr2.at[0], ((dp + i) % 8, ex), device_id_type=MESH)

    def member(p, k, i):
        return group(k, i) if p == 1 else group(i, k)

    def rhalf(s, p, j, way, k=0):
        a = ORDER[p][s]
        b = blk(shift(origin(s, p, j), a, 2))
        rows = half_rows(p, way)
        sem = slot(2, k) if s == 2 else slot(s, j)
        return pltpu.make_async_remote_copy(
            G.at[0, b, rows], G.at[1, BASE[s] + j, rows], sent.at[sent_sem(0, p, way)],
            fr.at[full_sem(0, p, way, sem)], nbr[a][way], device_id_type=MESH)

    def rfull(s, p, j, way, k=0):
        a = ORDER[p][s]
        b = blk(shift(origin(s, p, j), a, 1 if way == 0 else 3))
        rows = part_rows(p)
        sem = slot(2, k) if s == 2 else slot(s, j)
        return pltpu.make_async_remote_copy(
            G.at[0, b, rows], G.at[1, 21 + (BASE[s] + j) * 2 + way, rows], sent.at[sent_sem(0, p, way)],
            fr.at[full_sem(1, p, way, sem)], nbr[a][way], device_id_type=MESH)

    def add_half(s, p, j, way, f=0):
        k = blk(shift(origin(s, p, j), ORDER[p][s], 1 if way == 0 else 3))
        rows = half_rows(p, way)
        G[0, k, rows] = (G[0, k, rows].astype(F32) + G[1, BASE[s] + j, rows].astype(F32)).astype(BF)
        rfull(s, p, j, way, f).start()

    def add_full(s, p, j):
        k = blk(origin(s, p, j))
        rows = part_rows(p)
        f = 21 + (BASE[s] + j) * 2
        G[0, k, rows] = (G[0, k, rows].astype(F32) + (
            G[1, f, rows].astype(F32) + G[1, f + 1, rows].astype(F32))).astype(BF)

    def start2(p, k):
        def one(i):
            rhalf(2, p, member(p, k, i), 0, k).start()
            rhalf(2, p, member(p, k, i), 1, k).start()
        loop(0, 4, one)

    def halves_in(p, k):
        for w in range(2):
            settle(G.at[1, pl.ds(0, 4), half_rows(p, w)], fr.at[full_sem(0, p, w, slot(2, k))])

    def pass_on(p, k, i, f):
        for w in range(2):
            add_half(2, p, member(p, k, i), w, f)

    def mid2(p, step):
        if step == 0:
            halves_in(p, 2)
            loop(0, 4, lambda i: pass_on(p, 2, (i + 2) % 4, 0))
        elif step == 1:
            halves_in(p, 3)
            loop(1, 4, lambda i: pass_on(p, 3, i, 1))
        elif step == 2:
            halves_in(p, 1)
            loop(1, 4, lambda i: pass_on(p, 1, i, 1))
        elif step == 3:
            halves_in(p, 0)
            pass_on(p, 0, 2, 2)
        elif step == 4:
            odd(lambda k: pass_on(p, k, 0, 3))
            odd(lambda i: pass_on(p, 0, i, 3))
        else:
            pass_on(p, 0, 0, 4)

    def end2(p, f):
        n = (4, 6, 1, 4, 1)[f]
        for w in range(2):
            settle(G.at[1, pl.ds(0, n), part_rows(p)], fr.at[full_sem(1, p, w, slot(2, f))])
        take = lambda k, i: add_full(2, p, member(p, k, i))
        if f == 0:
            loop(0, 4, lambda i: take(2, i))
        elif f == 1:
            odd(lambda k: loop(1, 4, lambda i: take(k, i)))
        elif f == 2:
            take(0, 2)
        elif f == 3:
            odd(lambda k: take(k, 0))
            odd(lambda i: take(0, i))
        else:
            take(0, 0)

    def start(s, p, j):
        for w in range(2):
            rhalf(s, p, j, w).start()

    def mid(s, p, j):
        for w in range(2):
            rhalf(s, p, j, w).wait_recv()
            add_half(s, p, j, w)

    def end(s, p, j):
        for w in range(2):
            rfull(s, p, j, w).wait_recv()
        add_full(s, p, j)

    far = (2, 3, 1, 0)
    for i in range(1, 16):
        meta_copy(i).start()
    ev0 = gather_events(0)
    ev1 = early_events(1)
    ev0[0]()
    fetch_weights()
    ev0[1]()
    ev0[2]()
    ev0[3]()
    settle(META.at[pl.ds(0, 15)], mr.at[0])
    settle(META.at[pl.ds(0, 15)], ms.at[0])
    ev1[0]()
    ev0[4]()
    ev0[5]()
    ev1[1]()
    ev0[6]()
    prepare()
    ev1[2]()
    ev0[7]()
    ev1[3]()
    ev0[8]()
    ev1[4]()
    ev0[9]()
    ev1[5]()
    ev0[10]()
    ev1[6]()
    ev0[11]()
    for b in (0, 1, 3, 2):
        late_sends(1, b)
    gather_rest(0)
    loop(0, 4, lambda q: select(0, q))
    hop_bundle(1, 0)
    loop(4, 8, lambda q: select(0, q))
    settle_weights()
    hop_bundle(1, 1)
    loop(0, 2, gate_up)
    hop_bundle(1, 3)
    loop(2, 4, gate_up)
    loop(0, 2, hidden)
    hop_bundle(1, 2)
    loop(2, 4, hidden)
    gather_rest(1)
    loop(0, 8, lambda q: select(1, q))
    all_sent(0)
    all_sent(1)
    for a in range(3):
        for n in nbr[a]:
            pl.semaphore_signal(ready, inc=1, device_id=n, device_id_type=MESH)
    loop(0, 4, down)
    loop(0, 4, middle)
    loop(0, 4, lambda n: swap_d(n).wait_recv())

    def columns(b):
        y = (pos[1] + b) % 4
        loop(0, 4, lambda n: grad_x(n, y))
        loop(0, 8, lambda q: scatter(q, y))

    columns(2)
    pl.semaphore_wait(ready, 6)
    start2(0, 2)
    start2(1, 2)
    start2(2, 2)
    columns(3)
    start2(0, 3)
    start2(1, 3)
    start2(2, 3)
    columns(1)
    start2(0, 1)
    start2(1, 1)
    start2(2, 1)
    for p in range(3):
        mid2(p, 0)
    columns(0)
    start2(0, 0)
    start2(1, 0)
    start2(2, 0)
    for p in range(3):
        end2(p, 0)
        if p == 1:
            start(1, 1, 2)
        else:
            loop(0, 4, lambda a, p=p: start(1, p, (a + 2) % 4))
    for p in range(3):
        mid2(p, 1)
    for p in range(3):
        mid2(p, 2)
    mid(1, 1, 2)
    for p in range(3):
        mid2(p, 3)
    gate_tokens()
    for i in range(1, 16):
        gate_one(i).start()
    settle(HID.at[:, pl.ds(0, 192)], th.at[0])
    loop(0, 4, grad_down)
    for p in range(3):
        end2(p, 1)
        if p == 1:
            odd(lambda a: start(1, 1, a))
        else:
            loop(1, 4, lambda a, p=p: mid(1, p, a))
    for p in range(3):
        mid2(p, 4)
    settle(GR.at[pl.ds(0, 15)], gr1.at[0])
    acc = GS[ex]
    for i in range(1, 16):
        acc = acc + GR[i]
    GT[...] = acc
    for i in range(1, 8):
        gate_two(i).start()
    for p in range(3):
        end2(p, 2)
        if p == 1:
            start(1, 1, 0)
        end(1, p, 2)
        start(0, p, 0)
    for p in range(3):
        mid2(p, 5)
    odd(lambda a: mid(1, 1, a))
    for p in range(3):
        end2(p, 3)
        mid(1, p, 0)
        odd(lambda a, p=p: end(1, p, a))
        mid(0, p, 0)
    for p in range(3):
        end2(p, 4)
        end(1, p, 0)
    settle(GX.at[pl.ds(0, 7)], gr2.at[0])
    acc = GT[...]
    for i in range(1, 8):
        acc = acc + GX[i]
    gates[...] = acc / gpt[...]
    for p in range(3):
        end(0, p, 0)
    for c in range(4):
        dxo[:, c * 128:(c + 1) * 128] = G[0, me, c * 128:(c + 1) * 128, :]
    all_sent(0)
    settle(GR.at[pl.ds(0, 15)], gs1.at[0])
    settle(GX.at[pl.ds(0, 7)], gs2.at[0])
    settle(SND, es.at[0])
    settle(DT.at[:, :, pl.ds(0, 384)], ts.at[0])
    settle(HID.at[:, pl.ds(0, 192)], ts.at[1])
    for sem in (ol, osnd, orcv):
        settle(XS.at[:, pl.ds(0, 192)], sem.at[0])


def store_kernel(gd, dx, gt, gdo, dxo, gto, B, DB, GB, arrive, leave):
    pairs = [(gd.at[i // 4, pl.ds(i % 4 * 48, 48)], B.at[i], gdo.at[i // 4, pl.ds(i % 4 * 48, 48)]) for i in range(16)]
    pairs += [(dx, DB, dxo), (gt, GB, gto)]
    for i, (src, buf, dst) in enumerate(pairs):
        pltpu.make_async_copy(src, buf, arrive.at[i]).start()
    for i, (src, buf, dst) in enumerate(pairs):
        pltpu.make_async_copy(src, buf, arrive.at[i]).wait()
        pltpu.make_async_copy(buf, dst, leave.at[i]).start()
    for i, (src, buf, dst) in enumerate(pairs):
        pltpu.make_async_copy(buf, dst, leave.at[i]).wait()


def on_device(
    tokens, grad_out, expert_ids, gate_probs, seq_ids, log_ratio, advantages, w_gate, w_up, w_down
):
    vmem = pl.BlockSpec(memory_space=pltpu.VMEM)
    hbm = pl.BlockSpec(memory_space=pl.ANY)
    dma = lambda n: pltpu.SemaphoreType.DMA((n,))
    dx, gates, gd = pl.pallas_call(
        step_kernel,
        out_shape=(
            jax.ShapeDtypeStruct((128, 512), BF),
            jax.ShapeDtypeStruct((8, 128), F32),
            jax.ShapeDtypeStruct((4, 192, 4096), BF),
        ),
        in_specs=[pl.BlockSpec(memory_space=pltpu.SMEM)] + [vmem] * 6 + [hbm] * 3,
        out_specs=(vmem, vmem, hbm),
        scratch_shapes=[
            pltpu.VMEM((2, 64, 512, 128), BF),
            pltpu.VMEM((4, 384, 2048), BF),
            pltpu.VMEM((4, 384, 2048), BF),
            pltpu.VMEM((4, 1152, 2048), BF),
            pltpu.VMEM((4, 576, 384), F32),
            pltpu.VMEM((4, 576, 384), BF),
            pltpu.VMEM((4, 576, 384), BF),
            pltpu.VMEM((4, 384, 768), BF),
            pltpu.VMEM((4, 384, 384), BF),
            pltpu.VMEM((8, 192, 256), BF),
            pltpu.VMEM((8, 256, 192), BF),
            pltpu.VMEM((8, 192, 128), F32),
            pltpu.VMEM((16, 24, 128), F32),
            pltpu.VMEM((4, 8, 384), F32),
            pltpu.VMEM((16, 8, 128), F32),
            pltpu.VMEM((16, 8, 128), F32),
            pltpu.VMEM((8, 128), F32),
            pltpu.VMEM((8, 8, 128), F32),
            dma(2), dma(12), dma(120), dma(72), dma(1), dma(1), dma(1), dma(1), dma(1),
            dma(1), dma(8), dma(2), dma(4), dma(1), dma(1), dma(1), dma(1), dma(1), dma(1), dma(1), dma(1),
            pltpu.SemaphoreType.REGULAR,
        ],
        compiler_params=pltpu.CompilerParams(
            collective_id=0, has_side_effects=True, vmem_limit_bytes=67043328),
        name="expert_step",
    )(
        advantages, tokens, grad_out, expert_ids.T, gate_probs.T, seq_ids.reshape(1, -1), log_ratio.reshape(1, -1),
        w_gate, w_up, w_down)
    gd, dx, gates = pl.pallas_call(
        store_kernel,
        out_shape=(
            jax.ShapeDtypeStruct((4, 192, 4096), BF),
            jax.ShapeDtypeStruct((128, 512), BF),
            jax.ShapeDtypeStruct((8, 128), F32),
        ),
        in_specs=[hbm] * 3,
        out_specs=(hbm,) * 3,
        scratch_shapes=[
            pltpu.VMEM((16, 48, 4096), BF), pltpu.VMEM((128, 512), BF), pltpu.VMEM((8, 128), F32), dma(18), dma(18),
        ],
        name="store_results",
    )(gd, dx, gates)
    return dx, gates.T, gd


def solution(mesh):
    return jax.shard_map(
        on_device,
        mesh=mesh,
        in_specs=(
            P("expert", "dp"),
            P("expert", "dp"),
            P("expert", None),
            P("expert", None),
            P("expert"),
            P("expert"),
            P(),
            P("expert", "dp", None),
            P("expert", "dp", None),
            P("expert", "dp", None),
        ),
        out_specs=(P("expert", "dp"), P("expert", None), P("expert", "dp", None)),
        check_vma=False,
    )
```
